256 devices in a mesh: sec: 2 (over y_hi), dev: 128 (over y_lo, x, z, core).
Axes of the slice: x: 4, y: 4 (y_hi: 2, y_lo: 2; y = y_hi * 2 + y_lo), z: 8, core: 2. Of those that a mesh axis runs over, the one named last changes fastest.
Arguments:
- hidden_in: bfloat16 [2, 1024, 6144], P(None, ('sec', 'dev')), may hold values from -30 to 30
- queries: bfloat16 [2, 1024, 6144], P(None, ('sec', 'dev')), may hold values from -5.2 to 5.2
- new_entries: bfloat16 [2, 1024, 2048], P(None, ('sec', 'dev')), may hold values from -5.2 to 5.2
- request_cache_rows: bfloat16 [1024, 192, 2048], P(('sec', 'dev')), may hold values from -5.2 to 5.2
- lengths: int32 [1024], P(('sec', 'dev')), may hold values from 1 to 192, as said below
- expert_ids: int32 [2, 1024, 2], P(None, ('sec', 'dev')), may hold values from 0 to 7, all different within a row; in each aligned block of 4 rows (0 to 3, 4 to 7, ..., all dimensions but the last counted through in order) at most 2 rows name the same one
- route_weights: float32 [2, 1024, 2], P(None, ('sec', 'dev')), may hold values from 0.25 to 1
- gate_weight: bfloat16 [2, 32768, 6144], P('sec', 'dev'), may hold values from -0.078125 to 0.078125
- up_weight: bfloat16 [2, 32768, 6144], P('sec', 'dev'), may hold values from -0.078125 to 0.078125
- down_weight: bfloat16 [2, 32768, 6144], P('sec', 'dev'), may hold values from -0.0625 to 0.0625
Outputs:
- attended: bfloat16 [2, 1024, 6144], P(None, ('sec', 'dev'))
- expert_mix: bfloat16 [2, 1024, 6144], P(None, ('sec', 'dev'))
The draws below stay inside these ranges and needn't reach their ends.
Inputs may be any that keep to these rules, and one draw needn't show every extreme that they name: `lengths`: some request has exactly 192 cached positions. `expert_ids`: the two experts of a token differ. Among one device's tokens of one step (aligned blocks of 4 rows), no expert is named more than 2 times, a bound that some block reaches.
All inputs are finite; a program needn't handle non-finite values.
Results may differ from the reference program's by a relative error of at most 0.008.
Values may be sent and summed in bfloat16 or wider, within the bound.
A program may use at most 128 MiB of HBM per device.

```python
import math
import jax
import jax.numpy as jnp
import numpy as np
from jax import lax

D = 6144
QUERY_HEADS = 48
KEY_VALUE_HEADS = 8
HEAD_SIZE = 128
E = 8
FF = 8192
LONGEST_LENGTH = 192
REQ_DEV = 4
CAP = 2
REQUEST_COUNT = 1024
GROUPS = 16
HID_DEV = 256
N_SEC = 2
N_DEV = 128


def draw_hidden_in(key, part):
    own = jax.random.fold_in(key, 4)
    first, second, third_part = jax.random.split(own, 3)
    row_scale = jnp.exp(jax.random.uniform(first, (2, REQUEST_COUNT, 1), minval=0.0, maxval=math.log(10.0)))
    column_scale = jnp.exp(jax.random.uniform(second, (1, 1, D), minval=0.0, maxval=math.log(10.0)))
    basis = jnp.clip(jax.random.normal(third_part, (2, REQUEST_COUNT, D)), -3.0, 3.0)
    return (basis * row_scale * column_scale / 10.0).astype(jnp.bfloat16)


def draw_queries(key, part):
    own = jax.random.fold_in(key, 2)
    values = jnp.clip(jax.random.normal(own, (2, REQUEST_COUNT, QUERY_HEADS * HEAD_SIZE)), -4.0, 4.0)
    return values.astype(jnp.bfloat16)


def draw_new_entries(key, part):
    own = jax.random.fold_in(key, 3)
    key_row_width = KEY_VALUE_HEADS * HEAD_SIZE
    values = jnp.clip(jax.random.normal(own, (2, REQUEST_COUNT, 2 * key_row_width)), -4.0, 4.0)
    return values.astype(jnp.bfloat16)


def draw_request_cache_rows(key, part):
    own = jax.random.fold_in(key, 1)
    key_row_width = KEY_VALUE_HEADS * HEAD_SIZE
    values = jnp.clip(jax.random.normal(own, (REQUEST_COUNT, LONGEST_LENGTH, 2 * key_row_width)), -4.0, 4.0)
    return values.astype(jnp.bfloat16)


def draw_lengths(key, part):
    first, second = jax.random.split(jax.random.fold_in(key, 5))
    drawn = jax.random.randint(first, (REQUEST_COUNT,), 1, LONGEST_LENGTH + 1)
    picked = jax.random.randint(second, (), 0, REQUEST_COUNT)
    return jnp.where(jnp.arange(REQUEST_COUNT) == picked, LONGEST_LENGTH, drawn).astype(jnp.int32)


def block_levels(stream_key, shape, pieces, low, top_value):
    def one(dim, parts):
        draws = jax.random.uniform(jax.random.fold_in(jax.random.fold_in(stream_key, 6), dim), (parts,), jnp.float32, low / len(pieces), top_value / len(pieces))
        return jnp.repeat(jnp.exp(draws), shape[dim] // parts).reshape((-1,) + (1,) * (len(shape) - dim - 1))

    loudness = one(*pieces[0])
    for cut in pieces[1:]:
        loudness = loudness * one(*cut)
    return loudness


def assign_block(stream_key, own, number, rows, number_of, top, limit, skew):
    sequence = jax.random.permutation(stream_key, number_of)
    heavy_load, ordinary = load_shares(number_of, rows * top, limit, skew, True), load_shares(number_of, rows * top, limit, skew, False)
    places = jnp.arange(number_of)

    def named(sizes, turn):
        used = int((sizes > 0).sum())
        fixed = max(1, used // 4)
        shifted = fixed + (places - fixed + turn * (used - fixed)) % max(1, number_of - fixed)
        return jnp.zeros((number_of,), jnp.int32).at[sequence[jnp.where(places < fixed, places, shifted)]].set(jnp.asarray(sizes, jnp.int32))

    sizes = jnp.where(number % 4 == 0, named(heavy_load, number // 4), named(ordinary, number - number // 4 - 1))
    mixed = jax.random.permutation(jax.random.fold_in(own, 3), number_of)
    giver, sink = mixed[0:number_of // 2 * 2:2], mixed[1:number_of // 2 * 2:2]
    margin = jnp.minimum(sizes[giver] - 1, limit - sizes[sink]) // 2
    margin = jnp.where((giver == sequence[0]) | (sink == sequence[0]) | (sizes[sink] == 0), 0, jnp.maximum(margin, 0))
    shifted = jax.random.randint(jax.random.fold_in(own, 4), (number_of // 2,), 0, 1 << 20) % (margin + 1)
    sizes = sizes.at[giver].add(-shifted).at[sink].add(shifted)
    labels = jnp.searchsorted(jnp.cumsum(sizes), jnp.arange(rows * top), side="right").astype(jnp.int32)
    listing = labels.reshape(top, rows).T
    listing = listing[jax.random.permutation(jax.random.fold_in(own, 1), rows)]
    turn = jax.random.randint(jax.random.fold_in(own, 2), (rows, 1), 0, top)
    return jnp.take_along_axis(listing, (jnp.arange(top)[None, :] + turn) % top, axis=1)


def load_shares(amount, total, reach, slope, full):
    loads = [(1 << 20) // math.isqrt(rank ** slope) + 1 for rank in range(1, amount + 1)]
    largest = reach if full else min(reach, max(-(-total // amount), total * loads[0] // sum(loads)))
    least = 1 if total - largest >= amount - 1 else 0
    counts, rest = [largest] + [least] * (amount - 1), total - largest - least * (amount - 1)
    while rest > 0:
        movable = [i for i in range(1, amount) if counts[i] < largest] or [i for i in range(1, amount) if counts[i] < reach]
        whole, budget = sum([loads[i] for i in movable]), rest
        for i in movable:
            more = min(reach - counts[i], max(1, budget * loads[i] // whole), rest)
            counts[i] = counts[i] + more
            rest = rest - more
    return np.array(counts)


def gaussian(own_key, shape, scale, reach, shards=(), held_as=jnp.bfloat16):
    values = jax.random.normal(own_key, shape, jnp.float32) * scale
    if len(shards) > 0:
        values = block_levels(own_key, shape, shards, -0.22, 0.18) * values
    return jnp.clip(values, min=-reach, max=reach).astype(held_as)


def setup_inputs(seed: int = 0) -> dict:
    splits = jax.random.split(jax.random.key(seed), 11)
    hidden_in = draw_hidden_in(jax.random.fold_in(splits[10], 71), 0)
    queries = draw_queries(jax.random.fold_in(splits[10], 71), 0)
    new_entries = draw_new_entries(jax.random.fold_in(splits[10], 71), 0)
    request_cache_rows = draw_request_cache_rows(jax.random.fold_in(splits[10], 71), 0)
    lengths = draw_lengths(jax.random.fold_in(splits[10], 71), 0)
    expert_ids_keys = jax.random.split(jax.random.fold_in(splits[5], 1), 2 * REQUEST_COUNT // REQ_DEV)
    expert_ids_turns = jax.random.permutation(jax.random.fold_in(splits[5], 3), 2 * REQUEST_COUNT // REQ_DEV)
    expert_ids = jax.vmap(lambda own, number: assign_block(jax.random.fold_in(splits[5], 2), own, number, REQ_DEV, E, 2, CAP, 2))(expert_ids_keys, expert_ids_turns).reshape((2, REQUEST_COUNT, 2))
    route_weights = jnp.clip(0.25 + 0.75 * jax.random.uniform(splits[6], (2, REQUEST_COUNT, 2), jnp.float32) ** block_levels(splits[6], (2, REQUEST_COUNT, 2), ((1, 256),), -0.2, 0.2), 0.25, 1.0)
    gate_weight = gaussian(splits[7], (2, E * FF // 2, D), D ** -0.5, 0.078125, ((0, 2), (1, 128)))
    up_weight = gaussian(splits[8], (2, E * FF // 2, D), D ** -0.5, 0.078125, ((0, 2), (1, 128)))
    down_weight = gaussian(splits[9], (2, E * FF // 2, D), FF ** -0.5, 0.0625, ((0, 2), (1, 128)))
    return dict(hidden_in=hidden_in, queries=queries, new_entries=new_entries, request_cache_rows=request_cache_rows, lengths=lengths, expert_ids=expert_ids, route_weights=route_weights, gate_weight=gate_weight, up_weight=up_weight, down_weight=down_weight)


def attend_all(decode_step_index, queries, new_entries, request_cache_rows, lengths):
    key_row_width = KEY_VALUE_HEADS * HEAD_SIZE
    query_group_width = QUERY_HEADS // KEY_VALUE_HEADS
    scale_factor = 1.0 / math.sqrt(HEAD_SIZE)
    query_every_step = queries[decode_step_index].reshape(REQUEST_COUNT, KEY_VALUE_HEADS, query_group_width, HEAD_SIZE)
    fresh_all = jnp.transpose(new_entries[:decode_step_index + 1], (1, 0, 2))

    def single(items):
        query_one, single_cache, newest_single, length_one = items
        cached_key_rows = single_cache[:, :key_row_width].reshape(LONGEST_LENGTH, KEY_VALUE_HEADS, HEAD_SIZE).astype(jnp.float32)
        cached_value_rows = single_cache[:, key_row_width:].reshape(LONGEST_LENGTH, KEY_VALUE_HEADS, HEAD_SIZE).astype(jnp.float32)
        newest_keys = newest_single[:, :key_row_width].reshape(-1, KEY_VALUE_HEADS, HEAD_SIZE).astype(jnp.float32)
        newest_values = newest_single[:, key_row_width:].reshape(-1, KEY_VALUE_HEADS, HEAD_SIZE).astype(jnp.float32)
        query_float = query_one.astype(jnp.float32)
        past_scores = jnp.einsum('gqd,pgd->gqp', query_float, cached_key_rows) * scale_factor
        visible = jnp.arange(LONGEST_LENGTH) < length_one
        past_scores = jnp.where(visible[None, None, :], past_scores, -jnp.inf)
        fresh_scores = jnp.einsum('gqd,sgd->gqs', query_float, newest_keys) * scale_factor
        row_max = jnp.maximum(lax.optimization_barrier(jnp.max(past_scores, axis=-1)), lax.optimization_barrier(jnp.max(fresh_scores, axis=-1)))[..., None]
        past_exp = jnp.exp(past_scores - row_max)
        fresh_exp = jnp.exp(fresh_scores - row_max)
        exp_sum = lax.optimization_barrier(jnp.sum(past_exp, axis=-1, keepdims=True)) + lax.optimization_barrier(jnp.sum(fresh_exp, axis=-1, keepdims=True))
        past_weight = lax.optimization_barrier((past_exp / exp_sum).astype(jnp.bfloat16)).astype(jnp.float32)
        fresh_weight = lax.optimization_barrier((fresh_exp / exp_sum).astype(jnp.bfloat16)).astype(jnp.float32)
        mixed_heads = jnp.einsum('gqp,pgd->gqd', past_weight, cached_value_rows)
        mixed_heads = mixed_heads + jnp.einsum('gqs,sgd->gqd', fresh_weight, newest_values)
        return mixed_heads.reshape(QUERY_HEADS * HEAD_SIZE).astype(jnp.bfloat16)
    return lax.map(single, (query_every_step, request_cache_rows, fresh_all, lengths))

def reference(hidden_in, queries, new_entries, request_cache_rows, lengths, expert_ids, route_weights, gate_weight, up_weight, down_weight):
    sources = N_SEC * N_DEV
    half_units = FF // 2
    gate_full = gate_weight.reshape(2, E, half_units, D)
    up_full = up_weight.reshape(2, E, half_units, D)
    down_full = down_weight.reshape(2, E, half_units, D)
    contract = (((1,), (1,)), ((), ()))
    attended_list = []
    mix_list = []
    for decode_step_index in range(2):
        attended_now = attend_all(decode_step_index, queries, new_entries, request_cache_rows, lengths)
        residual_sum = hidden_in[decode_step_index].astype(jnp.float32) + attended_now.astype(jnp.float32)
        mean_square = lax.optimization_barrier(jnp.mean(residual_sum * residual_sum, axis=-1, keepdims=True))
        normed = (residual_sum * lax.rsqrt(mean_square + 1e-05)).astype(jnp.bfloat16)
        choices_flat = expert_ids[decode_step_index].reshape(sources, 2 * REQ_DEV)
        onehot = (choices_flat[:, :, None] == jnp.arange(E)[None, None, :]).astype(jnp.int32)
        earlier = jnp.cumsum(onehot, axis=1) - onehot
        position = choices_flat * CAP + lax.optimization_barrier(jnp.sum(earlier * onehot, axis=2))
        selector = (jnp.arange(E * CAP)[None, :, None] == position[:, None, :]).astype(jnp.float32)
        doubled = jnp.repeat(normed.reshape(sources, REQ_DEV, D), 2, axis=1).astype(jnp.float32)
        filled = jnp.einsum('pkr,prd->pkd', selector, doubled).astype(jnp.bfloat16)
        filled = filled.reshape(sources, E, CAP, D)

        def run_expert(index):
            rows = jnp.take(filled, index, axis=1).reshape(sources * CAP, D)
            gate_rows = jnp.take(gate_full, index, axis=1).reshape(FF, D)
            up_rows = jnp.take(up_full, index, axis=1).reshape(FF, D)
            down_rows = jnp.take(down_full, index, axis=1).reshape(2, GROUPS, HID_DEV, D)
            gate_part = lax.dot_general(rows, gate_rows, contract, preferred_element_type=jnp.float32)
            up_part = lax.dot_general(rows, up_rows, contract, preferred_element_type=jnp.float32)
            activated = (jax.nn.silu(gate_part) * up_part).astype(jnp.bfloat16)
            activated = activated.reshape(sources * CAP, 2, GROUPS, HID_DEV)

            def add_block(running, block):
                first_half = jnp.dot(activated[:, 0, block], down_rows[0, block], preferred_element_type=jnp.float32).astype(jnp.bfloat16)
                second_half = jnp.dot(activated[:, 1, block], down_rows[1, block], preferred_element_type=jnp.float32).astype(jnp.bfloat16)
                first_half = lax.optimization_barrier(first_half)
                second_half = lax.optimization_barrier(second_half)
                pair_value = (first_half.astype(jnp.float32) + second_half.astype(jnp.float32)).astype(jnp.bfloat16)
                pair_value = lax.optimization_barrier(pair_value)
                return (running + pair_value.astype(jnp.float32), None)
            running, unused = lax.scan(add_block, jnp.zeros((sources * CAP, D), jnp.float32), jnp.arange(GROUPS))
            return running.reshape(sources, CAP, D)
        expert_out = lax.map(run_expert, jnp.arange(E))
        flat_out = jnp.transpose(expert_out, (1, 0, 2, 3)).reshape(sources, E * CAP, D)
        picked = jnp.take_along_axis(flat_out, position[:, :, None], axis=1).reshape(REQUEST_COUNT, 2, D)
        weights_now = route_weights[decode_step_index].astype(jnp.float32)
        mixture = picked[:, 0] * weights_now[:, 0:1] + picked[:, 1] * weights_now[:, 1:2]
        attended_list.append(attended_now)
        mix_list.append(mixture.astype(jnp.bfloat16))
    return (jnp.stack(attended_list), jnp.stack(mix_list))
```

```python
import functools
import math

import jax
import jax.numpy as jnp
from jax import lax
from jax.experimental import pallas as pl
from jax.experimental.pallas import tpu as pltpu
from jax.sharding import PartitionSpec as P

QUERY_HEADS = 48
KEY_VALUE_HEADS = 8
HEAD_SIZE = 128
E = 8
LONGEST_LENGTH = 192
CAP = 2
STEPS = 2
GROUP = QUERY_HEADS // KEY_VALUE_HEADS
PADDED_GROUP = 8
FRESH_ROWS = 16
RING = 8
LANE = 2 * RING
SLOTS = STEPS * CAP
MESH = pl.DeviceIdType.MESH
CONTRACT_LAST = (((1,), (1,)), ((), ()))


def attend_kernel(lengths_ref, q_ref, fresh_ref, cache_ref, out_ref):
    rows = STEPS * PADDED_GROUP
    key_width = KEY_VALUE_HEADS * HEAD_SIZE
    scale = 1.0 / math.sqrt(HEAD_SIZE)
    length = lengths_ref[pl.program_id(0)]
    visible = lax.broadcasted_iota(jnp.int32, (rows, LONGEST_LENGTH), 1) < length
    row = lax.broadcasted_iota(jnp.int32, (rows, FRESH_ROWS), 0)
    column = lax.broadcasted_iota(jnp.int32, (rows, FRESH_ROWS), 1)
    fresh_visible = column <= row // PADDED_GROUP
    for head in range(KEY_VALUE_HEADS):
        keys = pl.ds(head * HEAD_SIZE, HEAD_SIZE)
        values = pl.ds(key_width + head * HEAD_SIZE, HEAD_SIZE)
        q = q_ref[0, head]
        past = lax.dot_general(
            q, cache_ref[0, :, keys], CONTRACT_LAST, preferred_element_type=jnp.float32
        )
        past = jnp.where(visible, past * scale, -jnp.inf)
        fresh = lax.dot_general(
            q, fresh_ref[0, :, keys], CONTRACT_LAST, preferred_element_type=jnp.float32
        )
        fresh = jnp.where(fresh_visible, fresh * scale, -jnp.inf)
        top = jnp.maximum(
            jnp.max(past, axis=1, keepdims=True), jnp.max(fresh, axis=1, keepdims=True)
        )
        past = jnp.exp(past - top)
        fresh = jnp.exp(fresh - top)
        total = jnp.sum(past, axis=1, keepdims=True) + jnp.sum(fresh, axis=1, keepdims=True)
        mixed = jnp.dot(
            (past / total).astype(jnp.bfloat16),
            cache_ref[0, :, values],
            preferred_element_type=jnp.float32,
        )
        mixed = mixed + jnp.dot(
            (fresh / total).astype(jnp.bfloat16),
            fresh_ref[0, :, values],
            preferred_element_type=jnp.float32,
        )
        out_ref[0, head] = mixed.astype(jnp.bfloat16)


def attend(queries, new_entries, request_cache_rows, lengths):
    requests = queries.shape[1]
    rows = STEPS * PADDED_GROUP
    width = request_cache_rows.shape[2]
    q = queries.reshape(STEPS, requests, KEY_VALUE_HEADS, GROUP, HEAD_SIZE)
    q = jnp.pad(q, ((0, 0), (0, 0), (0, 0), (0, PADDED_GROUP - GROUP), (0, 0)))
    q = q.transpose(1, 2, 0, 3, 4).reshape(requests, KEY_VALUE_HEADS, rows, HEAD_SIZE)
    fresh = jnp.pad(new_entries.transpose(1, 0, 2), ((0, 0), (0, FRESH_ROWS - STEPS), (0, 0)))
    heads_spec = pl.BlockSpec(
        (1, KEY_VALUE_HEADS, rows, HEAD_SIZE), lambda r, lengths_ref: (r, 0, 0, 0)
    )
    out = pl.pallas_call(
        attend_kernel,
        out_shape=jax.ShapeDtypeStruct(q.shape, jnp.bfloat16),
        grid_spec=pltpu.PrefetchScalarGridSpec(
            num_scalar_prefetch=1,
            grid=(requests,),
            in_specs=[
                heads_spec,
                pl.BlockSpec((1, FRESH_ROWS, width), lambda r, lengths_ref: (r, 0, 0)),
                pl.BlockSpec((1, LONGEST_LENGTH, width), lambda r, lengths_ref: (r, 0, 0)),
            ],
            out_specs=heads_spec,
        ),
        name="attend",
    )(lengths, q, fresh, request_cache_rows)
    out = out.reshape(requests, KEY_VALUE_HEADS, STEPS, PADDED_GROUP, HEAD_SIZE)[:, :, :, :GROUP]
    return out.transpose(2, 0, 1, 3, 4).reshape(STEPS, requests, QUERY_HEADS * HEAD_SIZE)


def plane_kernel(sections, columns, in_ref, out_ref, send_sem, recv_sem, own_sem):
    pieces = in_ref.shape[0]
    count = sections * columns
    device = lax.axis_index("dev")
    lane = device % LANE
    me = lax.axis_index("sec") * columns + device // LANE

    def place(peer):
        return (peer // columns, (peer % columns) * LANE + lane)

    barrier = pltpu.get_barrier_semaphore()
    for offset in range(1, count):
        pl.semaphore_signal(
            barrier, inc=1, device_id=place((me + offset) % count), device_id_type=MESH
        )
    own = pltpu.make_async_copy(in_ref.at[me % pieces], out_ref.at[me], own_sem)
    own.start()
    pl.semaphore_wait(barrier, count - 1)
    copies = []
    for offset in range(1, count):
        peer = (me + offset) % count
        copy = pltpu.make_async_remote_copy(
            src_ref=in_ref.at[peer % pieces],
            dst_ref=out_ref.at[me],
            send_sem=send_sem.at[offset - 1],
            recv_sem=recv_sem.at[offset - 1],
            device_id=place(peer),
            device_id_type=MESH,
        )
        copy.start()
        copies.append(copy)
    own.wait()
    for copy in copies:
        copy.wait()


def exchange_in_plane(pieces, sections, columns, collective_id, name):
    count = sections * columns
    return pl.pallas_call(
        functools.partial(plane_kernel, sections, columns),
        out_shape=jax.ShapeDtypeStruct((count,) + pieces.shape[1:], pieces.dtype),
        in_specs=[pl.BlockSpec(memory_space=pl.ANY)],
        out_specs=pl.BlockSpec(memory_space=pl.ANY),
        scratch_shapes=[
            pltpu.SemaphoreType.DMA((count - 1,)),
            pltpu.SemaphoreType.DMA((count - 1,)),
            pltpu.SemaphoreType.DMA,
        ],
        compiler_params=pltpu.CompilerParams(
            collective_id=collective_id, has_side_effects=True
        ),
        name=name,
    )(pieces)


def experts_kernel(
    block_ref,
    gate_ref,
    up_ref,
    down_ref,
    out_ref,
    gate,
    up,
    down,
    rows_0,
    rows_mid,
    rows_4,
    part_0,
    part_mid,
    part_4,
    other_0,
    other_mid,
    other_4,
    ring_3,
    ring_mid,
    gate_sum,
    up_sum,
    hidden,
    load_sem,
    gather_send,
    gather_recv,
    share_send,
    share_recv,
    pair_send,
    pair_recv,
    reduce_send,
    reduce_recv,
):
    size = block_ref.shape[0]
    half = size // 2
    features = block_ref.shape[1]
    wide = min(1024, features)
    narrow = min(512, features)
    section = lax.axis_index("sec")
    device = lax.axis_index("dev")
    column, z, core = device // LANE, (device % LANE) // 2, device % 2

    def at_z(where):
        return (section, column * LANE + (where % RING) * 2 + core)

    ahead, behind = at_z(z + 1), at_z(z + RING - 1)
    partner = (section, device + 1 - 2 * core)
    onward = (ahead, behind)
    back = (behind, ahead)

    def remote(source, target, send_sem, recv_sem, where):
        return pltpu.make_async_remote_copy(
            src_ref=source,
            dst_ref=target,
            send_sem=send_sem,
            recv_sem=recv_sem,
            device_id=where,
            device_id_type=MESH,
        )

    loads = [
        pltpu.make_async_copy(block_ref, rows_0.at[pl.ds(0, size)], load_sem.at[0]),
        pltpu.make_async_copy(gate_ref.at[0], gate, load_sem.at[1]),
        pltpu.make_async_copy(up_ref.at[0], up, load_sem.at[2]),
        pltpu.make_async_copy(down_ref.at[0], down, load_sem.at[3]),
    ]
    for load in loads:
        load.start()
    barrier = pltpu.get_barrier_semaphore()
    for where in (ahead, behind, partner):
        pl.semaphore_signal(barrier, inc=1, device_id=where, device_id_type=MESH)
    pl.semaphore_wait(barrier, 3)
    loads[0].wait()
    sends = []

    def start(copy):
        copy.start()
        sends.append(copy)
        return copy

    def rows_at(k, direction, h, of_partner=0):
        if k == 0:
            return rows_0.at[pl.ds(of_partner * size + h * half, half)]
        if k == 4:
            return rows_4.at[pl.ds(of_partner * size + h * half, half)]
        return rows_mid.at[
            k - 1, pl.ds(direction * 2 * size + of_partner * size + h * half, half)
        ]

    def gather(k, direction, h):
        return remote(
            rows_at(k - 1, direction, h),
            rows_at(k, direction, h),
            gather_send.at[k - 1, direction, h],
            gather_recv.at[k - 1, direction, h],
            onward[direction],
        )

    def share(k, direction, h):
        return remote(
            rows_at(k, direction, h),
            rows_at(k, direction, h, 1),
            share_send.at[k, direction, h],
            share_recv.at[k, direction, h],
            partner,
        )

    def chunks(k):
        if k == 0:
            return [(0, 0), (0, 1)]
        if k == 4:
            return [(0, 0), (1, 1)]
        return [(0, 0), (1, 0), (0, 1), (1, 1)]

    def multiply(rows, part):
        count = rows.shape[0]

        def features_step(i, carry):
            at = pl.ds(pl.multiple_of(i * wide, wide), wide)
            x = rows[:, at]
            gate_sum[pl.ds(0, count)] += lax.dot_general(
                x, gate[:, at], CONTRACT_LAST, preferred_element_type=jnp.float32
            )
            up_sum[pl.ds(0, count)] += lax.dot_general(
                x, up[:, at], CONTRACT_LAST, preferred_element_type=jnp.float32
            )
            return carry

        gate_sum[...] = jnp.zeros_like(gate_sum)
        up_sum[...] = jnp.zeros_like(up_sum)
        lax.fori_loop(0, features // wide, features_step, 0)
        value = gate_sum[pl.ds(0, count)]
        value = value / (1.0 + jnp.exp(-value)) * up_sum[pl.ds(0, count)]
        hidden[pl.ds(0, count)] = value.astype(jnp.bfloat16)

        def output_step(i, carry):
            at = pl.ds(pl.multiple_of(i * wide, wide), wide)
            part[:, at] = jnp.dot(
                hidden[pl.ds(0, count)], down[:, at], preferred_element_type=jnp.float32
            ).astype(jnp.bfloat16)
            return carry

        lax.fori_loop(0, features // wide, output_step, 0)

    def pair(k, direction):
        if k == 0:
            source, target = part_0.at[pl.ds(size, size)], other_0
        elif k == 4:
            source, target = part_4.at[pl.ds(size, size)], other_4
        else:
            source = part_mid.at[k - 1, pl.ds(direction * 2 * size + size, size)]
            target = other_mid.at[k - 1, pl.ds(direction * size, size)]
        return remote(
            source, target, pair_send.at[k, direction], pair_recv.at[k, direction], partner
        )

    def part_at(k, direction, h):
        if k == 4:
            return part_4.at[pl.ds(h * half, half)]
        return part_mid.at[k - 1, pl.ds(direction * 2 * size + h * half, half)]

    def other_at(k, direction, h):
        if k == 4:
            return other_4.at[pl.ds(h * half, half)]
        return other_mid.at[k - 1, pl.ds(direction * size + h * half, half)]

    def ring_at(k, direction, h):
        if k == 3:
            return ring_3.at[direction]
        return ring_mid.at[k, pl.ds(direction * size + h * half, half)]

    def reduce(k, direction, h):
        return remote(
            part_at(k, direction, h),
            ring_at(k - 1, direction, h),
            reduce_send.at[k - 1, direction, h],
            reduce_recv.at[k - 1, direction, h],
            back[direction],
        )

    def add(target, sources):
        def step(i, carry):
            at = pl.ds(pl.multiple_of(i * narrow, narrow), narrow)
            total = sources[0][:, at].astype(jnp.float32)
            for source in sources[1:]:
                total = total + source[:, at].astype(jnp.float32)
            target[:, at] = total.astype(jnp.bfloat16)
            return carry

        lax.fori_loop(0, features // narrow, step, 0)

    for h in range(2):
        for direction in range(2):
            start(gather(1, direction, h))
        start(share(0, 0, h))
    for load in loads[1:]:
        load.wait()
    for h in range(2):
        share(0, 0, h).wait_recv()
    multiply(rows_0, part_0)
    start(pair(0, 0))

    for k in range(1, 5):
        for direction, h in chunks(k):
            gather(k, direction, h).wait_recv()
            if k < 3 or (k == 3 and h == direction):
                start(gather(k + 1, direction, h))
            start(share(k, direction, h))
        for direction, h in chunks(k):
            share(k, direction, h).wait_recv()
        if k == 4:
            multiply(rows_4, part_4)
            start(pair(4, 0))
        else:
            multiply(rows_mid.at[k - 1], part_mid.at[k - 1])
            for direction in range(2):
                start(pair(k, direction))
        if k == 3:
            for direction in range(2):
                pair(3, direction).wait_recv()
                h = 1 - direction
                add(
                    part_at(3, direction, h),
                    [part_at(3, direction, h), other_at(3, direction, h)],
                )
                start(reduce(3, direction, h))

    pair(4, 0).wait_recv()
    for direction in range(2):
        h = direction
        add(part_at(4, direction, h), [part_at(4, direction, h), other_at(4, direction, h)])
        start(reduce(4, direction, h))
    for k in range(3, 0, -1):
        if k < 3:
            for direction in range(2):
                pair(k, direction).wait_recv()
        for other_half in range(2):
            for direction in range(2):
                h = direction if other_half else 1 - direction
                if k == 3 and not other_half:
                    continue
                reduce(k + 1, direction, h).wait_recv()
                add(
                    part_at(k, direction, h),
                    [
                        part_at(k, direction, h),
                        other_at(k, direction, h),
                        ring_at(k, direction, h),
                    ],
                )
                start(reduce(k, direction, h))
    pair(0, 0).wait_recv()
    for h in range(2):
        for direction in range(2):
            reduce(1, direction, h).wait_recv()
    add(
        out_ref,
        [
            part_0.at[pl.ds(0, size)],
            other_0,
            ring_mid.at[0, pl.ds(0, size)],
            ring_mid.at[0, pl.ds(size, size)],
        ],
    )
    for copy in sends:
        copy.wait_send()


def run_experts(block, gate_weight, up_weight, down_weight):
    size, features = block.shape
    units = gate_weight.shape[1]
    half = size // 2
    bf16 = jnp.bfloat16
    anywhere = pl.BlockSpec(memory_space=pl.ANY)
    return pl.pallas_call(
        experts_kernel,
        out_shape=jax.ShapeDtypeStruct((size, features), bf16),
        in_specs=[anywhere] * 4,
        out_specs=pl.BlockSpec(memory_space=pltpu.VMEM),
        scratch_shapes=[
            pltpu.VMEM((units, features), bf16),
            pltpu.VMEM((units, features), bf16),
            pltpu.VMEM((units, features), bf16),
            pltpu.VMEM((2 * size, features), bf16),
            pltpu.VMEM((3, 4 * size, features), bf16),
            pltpu.VMEM((2 * size, features), bf16),
            pltpu.VMEM((2 * size, features), bf16),
            pltpu.VMEM((3, 4 * size, features), bf16),
            pltpu.VMEM((2 * size, features), bf16),
            pltpu.VMEM((size, features), bf16),
            pltpu.VMEM((3, 2 * size, features), bf16),
            pltpu.VMEM((size, features), bf16),
            pltpu.VMEM((2, half, features), bf16),
            pltpu.VMEM((3, 2 * size, features), bf16),
            pltpu.VMEM((4 * size, units), jnp.float32),
            pltpu.VMEM((4 * size, units), jnp.float32),
            pltpu.VMEM((4 * size, units), bf16),
            pltpu.SemaphoreType.DMA((4,)),
            pltpu.SemaphoreType.DMA((4, 2, 2)),
            pltpu.SemaphoreType.DMA((4, 2, 2)),
            pltpu.SemaphoreType.DMA((5, 2, 2)),
            pltpu.SemaphoreType.DMA((5, 2, 2)),
            pltpu.SemaphoreType.DMA((5, 2)),
            pltpu.SemaphoreType.DMA((5, 2)),
            pltpu.SemaphoreType.DMA((4, 2, 2)),
            pltpu.SemaphoreType.DMA((4, 2, 2)),
        ],
        compiler_params=pltpu.CompilerParams(
            collective_id=1, has_side_effects=True, vmem_limit_bytes=60 * 1024 * 1024
        ),
        name="experts",
    )(block, gate_weight, up_weight, down_weight)


def body(
    sections,
    columns,
    hidden_in,
    queries,
    new_entries,
    request_cache_rows,
    lengths,
    expert_ids,
    route_weights,
    gate_weight,
    up_weight,
    down_weight,
):
    requests, features = hidden_in.shape[1:]
    attended = attend(queries, new_entries, request_cache_rows, lengths)
    residual_sum = hidden_in.astype(jnp.float32) + attended.astype(jnp.float32)
    mean_square = jnp.mean(residual_sum * residual_sum, axis=-1, keepdims=True)
    normed = (residual_sum * lax.rsqrt(mean_square + 1e-05)).astype(jnp.bfloat16)

    choices = expert_ids.reshape(STEPS, 2 * requests)
    same = choices[:, :, None] == choices[:, None, :]
    earlier = jnp.tril(jnp.ones((2 * requests, 2 * requests), jnp.bool_), -1)
    rank = jnp.sum((same & earlier[None]).astype(jnp.int32), axis=2)
    slot = choices * SLOTS + jnp.arange(STEPS, dtype=jnp.int32)[:, None] * CAP + rank
    slot = slot.reshape(STEPS * requests, 2)
    targets = jnp.arange(E * SLOTS, dtype=jnp.int32)
    chosen = slot[:, :, None] == targets[None, None, :]
    selector = jnp.any(chosen, axis=1).astype(jnp.bfloat16)
    combine = jnp.sum(
        chosen.astype(jnp.float32) * route_weights.reshape(STEPS * requests, 2)[:, :, None], axis=1
    )
    outgoing = lax.dot_general(
        selector,
        normed.reshape(STEPS * requests, features),
        (((0,), (0,)), ((), ())),
        preferred_element_type=jnp.float32,
    ).astype(jnp.bfloat16)

    arrived = exchange_in_plane(
        outgoing.reshape(E, SLOTS, features), sections, columns, 0, "dispatch"
    )
    block = arrived.reshape(sections * columns * SLOTS, features)
    reduced = run_experts(block, gate_weight, up_weight, down_weight)
    returned = exchange_in_plane(
        reduced.reshape(sections * columns, SLOTS, features), sections, columns, 2, "collect"
    )
    summed = jnp.sum(
        returned.reshape(sections, columns * SLOTS, features).astype(jnp.float32), axis=0
    )
    mixture = jnp.dot(
        combine,
        summed,
        precision=lax.Precision.HIGHEST,
        preferred_element_type=jnp.float32,
    )
    return attended, mixture.astype(jnp.bfloat16).reshape(STEPS, requests, features)


def solution(mesh):
    sections, columns = mesh.shape["sec"], mesh.shape["dev"] // LANE
    placed = (
        P(None, ("sec", "dev"), None),
        P(None, ("sec", "dev"), None),
        P(None, ("sec", "dev"), None),
        P(("sec", "dev"), None, None),
        P(("sec", "dev")),
        P(None, ("sec", "dev"), None),
        P(None, ("sec", "dev"), None),
        P("sec", "dev", None),
        P("sec", "dev", None),
        P("sec", "dev", None),
    )
    return jax.shard_map(
        functools.partial(body, sections, columns),
        mesh=mesh,
        in_specs=placed,
        out_specs=(P(None, ("sec", "dev"), None), P(None, ("sec", "dev"), None)),
        check_vma=False,
    )
```

```python
import functools
import math

import jax
import jax.numpy as jnp
from jax import lax
from jax.experimental import pallas as pl
from jax.experimental.pallas import tpu as pltpu
from jax.sharding import PartitionSpec as P

QUERY_HEADS = 48
KEY_VALUE_HEADS = 8
HEAD_SIZE = 128
E = 8
LONGEST_LENGTH = 192
CAP = 2
STEPS = 2
GROUP = QUERY_HEADS // KEY_VALUE_HEADS
PADDED_GROUP = 8
RING = 8
LANE = 2 * RING
MESH = pl.DeviceIdType.MESH
CONTRACT_LAST = (((1,), (1,)), ((), ()))


def attend_kernel(lengths_ref, q_ref, fresh_ref, cache_ref, out_ref, cache, sem):
    requests = cache.shape[0]
    rows = STEPS * PADDED_GROUP
    key_width = KEY_VALUE_HEADS * HEAD_SIZE
    scale = 1.0 / math.sqrt(HEAD_SIZE)
    loads = [
        pltpu.make_async_copy(cache_ref.at[r], cache.at[r], sem.at[r]) for r in range(requests)
    ]
    for load in loads:
        load.start()
    every = KEY_VALUE_HEADS * rows
    place = lax.broadcasted_iota(jnp.int32, (every, LONGEST_LENGTH), 1)
    second = (lax.broadcasted_iota(jnp.int32, (every, 1), 0) // PADDED_GROUP) % STEPS == 1
    for r in range(requests):
        fresh_keys, fresh_values = [], []
        for t in range(STEPS):
            entry = fresh_ref[t, pl.ds(r, 1), :].astype(jnp.float32)
            fresh_keys.append(entry[:, :key_width])
            fresh_values.append(entry[:, key_width:])
        loads[r].wait()
        past, fresh = [], [[] for t in range(STEPS)]
        for head in range(KEY_VALUE_HEADS):
            lanes = slice(head * HEAD_SIZE, (head + 1) * HEAD_SIZE)
            q = q_ref[r, head]
            past.append(
                lax.dot_general(
                    q, cache[r, :, lanes], CONTRACT_LAST, preferred_element_type=jnp.float32
                )
            )
            wide = q.astype(jnp.float32)
            for t in range(STEPS):
                fresh[t].append(jnp.sum(wide * fresh_keys[t][:, lanes], axis=1, keepdims=True))
        past = jnp.concatenate(past, axis=0) * scale
        past = jnp.where(place < lengths_ref[r], past, -jnp.inf)
        fresh = [jnp.concatenate(part, axis=0) * scale for part in fresh]
        fresh[1] = jnp.where(second, fresh[1], -jnp.inf)
        top = jnp.maximum(jnp.max(past, axis=1, keepdims=True), jnp.maximum(fresh[0], fresh[1]))
        past = jnp.exp(past - top)
        fresh = [jnp.exp(part - top) for part in fresh]
        total = jnp.sum(past, axis=1, keepdims=True) + (fresh[0] + fresh[1])
        past = (past / total).astype(jnp.bfloat16)
        fresh = [(part / total).astype(jnp.bfloat16).astype(jnp.float32) for part in fresh]
        for head in range(KEY_VALUE_HEADS):
            lanes = slice(head * HEAD_SIZE, (head + 1) * HEAD_SIZE)
            values = slice(key_width + head * HEAD_SIZE, key_width + (head + 1) * HEAD_SIZE)
            here = slice(head * rows, (head + 1) * rows)
            mixed = jnp.dot(past[here], cache[r, :, values], preferred_element_type=jnp.float32)
            for t in range(STEPS):
                mixed = mixed + fresh[t][here] * fresh_values[t][:, lanes]
            out_ref[r, head] = mixed.astype(jnp.bfloat16)


def attend(queries, new_entries, request_cache_rows, lengths):
    requests = queries.shape[1]
    rows = STEPS * PADDED_GROUP
    q = queries.reshape(STEPS, requests, KEY_VALUE_HEADS, GROUP, HEAD_SIZE)
    q = jnp.pad(q, ((0, 0), (0, 0), (0, 0), (0, PADDED_GROUP - GROUP), (0, 0)))
    q = q.transpose(1, 2, 0, 3, 4).reshape(requests, KEY_VALUE_HEADS, rows, HEAD_SIZE)
    in_vmem = pl.BlockSpec(memory_space=pltpu.VMEM)
    out = pl.pallas_call(
        attend_kernel,
        out_shape=jax.ShapeDtypeStruct(q.shape, jnp.bfloat16),
        in_specs=[
            pl.BlockSpec(memory_space=pltpu.SMEM),
            in_vmem,
            in_vmem,
            pl.BlockSpec(memory_space=pl.ANY),
        ],
        out_specs=in_vmem,
        scratch_shapes=[
            pltpu.VMEM(request_cache_rows.shape, jnp.bfloat16),
            pltpu.SemaphoreType.DMA((requests,)),
        ],
        name="attend",
    )(lengths, q, new_entries, request_cache_rows)
    out = out.reshape(requests, KEY_VALUE_HEADS, STEPS, PADDED_GROUP, HEAD_SIZE)[:, :, :, :GROUP]
    return out.transpose(2, 0, 1, 3, 4).reshape(STEPS, requests, QUERY_HEADS * HEAD_SIZE)


def exchange_in_plane(
    sections, columns, both_out, own_out, both_in, own_in, send_sem, recv_sem, local_sem
):
    pieces = both_out.shape[0]
    count = sections * columns
    device = lax.axis_index("dev")
    lane = device % LANE
    section = lax.axis_index("sec")
    column = device // LANE
    me = section * columns + column
    copies = []

    def place(peer):
        return (peer // columns, (peer % columns) * LANE + lane)

    def greet():
        barrier = pltpu.get_barrier_semaphore()
        for offset in range(1, count):
            pl.semaphore_signal(
                barrier, inc=1, device_id=place((me + offset) % count), device_id_type=MESH
            )
        return lambda: pl.semaphore_wait(barrier, count - 1)

    def send(source, target, where):
        copies.append(
            pltpu.make_async_remote_copy(
                src_ref=source,
                dst_ref=target,
                send_sem=send_sem.at[len(copies)],
                recv_sem=recv_sem.at[len(copies)],
                device_id=where,
                device_id_type=MESH,
            )
        )
        copies[-1].start()

    def run():
        local = [
            pltpu.make_async_copy(both_out.at[me % pieces], both_in.at[me], local_sem.at[0]),
            pltpu.make_async_copy(own_out.at[column], own_in.at[column], local_sem.at[1]),
        ]
        for copy in local:
            copy.start()
        for offset in range(1, columns):
            peer = (column + offset) % columns
            send(own_out.at[peer], own_in.at[column], (section, peer * LANE + lane))
        for offset in range(1, count):
            peer = (me + offset) % count
            send(both_out.at[peer % pieces], both_in.at[me], place(peer))
        for copy in local + copies:
            copy.wait()

    return greet, run


def exchange_scratch(sections, columns, sent, features):
    count = sections * columns
    copies = count + columns - 2
    return [
        pltpu.VMEM((sent, CAP, features), jnp.bfloat16),
        pltpu.VMEM((columns, CAP, features), jnp.bfloat16),
        pltpu.VMEM((count, CAP, features), jnp.bfloat16),
        pltpu.VMEM((columns, CAP, features), jnp.bfloat16),
        pltpu.SemaphoreType.DMA((copies,)),
        pltpu.SemaphoreType.DMA((copies,)),
        pltpu.SemaphoreType.DMA((2,)),
    ]


def dispatch_kernel(
    sections, columns, attended_ref, hidden_ref, selector_ref, both_ref, own_ref, *scratch
):
    both_out, own_out, both_in, own_in = scratch[:4]
    greet, run = exchange_in_plane(sections, columns, *scratch)
    entered = greet()
    residual_sum = jnp.concatenate(
        [
            hidden_ref[t].astype(jnp.float32) + attended_ref[t].astype(jnp.float32)
            for t in range(STEPS)
        ],
        axis=0,
    )
    mean_square = jnp.mean(residual_sum * residual_sum, axis=-1, keepdims=True)
    normed = (residual_sum * lax.rsqrt(mean_square + 1e-05)).astype(jnp.bfloat16)
    slots = jnp.dot(selector_ref[...], normed, preferred_element_type=jnp.float32)
    slots = slots.astype(jnp.bfloat16)
    for e in range(columns):
        both_out[e] = slots[CAP * e : CAP * (e + 1)]
        own_out[e] = slots[CAP * (columns + e) : CAP * (columns + e + 1)]
    entered()
    run()
    for j in range(both_in.shape[0]):
        both_ref[pl.ds(CAP * j, CAP)] = both_in[j]
    for j in range(columns):
        own_ref[pl.ds(CAP * j, CAP)] = own_in[j]


def dispatch(attended, hidden_in, selector, sections, columns):
    features = attended.shape[-1]
    in_vmem = pl.BlockSpec(memory_space=pltpu.VMEM)
    return pl.pallas_call(
        functools.partial(dispatch_kernel, sections, columns),
        out_shape=(
            jax.ShapeDtypeStruct((sections * columns * CAP, features), jnp.bfloat16),
            jax.ShapeDtypeStruct((columns * CAP, features), jnp.bfloat16),
        ),
        in_specs=[in_vmem] * 3,
        out_specs=(in_vmem, in_vmem),
        scratch_shapes=exchange_scratch(sections, columns, columns, features),
        compiler_params=pltpu.CompilerParams(collective_id=0, has_side_effects=True),
        name="dispatch",
    )(attended, hidden_in, selector)


def collect_kernel(sections, columns, both_ref, own_ref, combine_ref, out_ref, rows, *scratch):
    both_out, own_out, both_in, own_in = scratch[:4]
    greet, run = exchange_in_plane(sections, columns, *scratch)
    entered = greet()
    for j in range(both_out.shape[0]):
        both_out[j] = both_ref[pl.ds(CAP * j, CAP)]
    for j in range(columns):
        own_out[j] = own_ref[pl.ds(CAP * j, CAP)]
    entered()
    run()
    count = both_in.shape[0]
    for j in range(count):
        rows[pl.ds(CAP * j, CAP)] = both_in[j]
    for j in range(columns):
        rows[pl.ds(CAP * (count + j), CAP)] = own_in[j]
    weights = combine_ref[...]
    parts = []
    for _ in range(3):
        part = weights.astype(jnp.bfloat16)
        weights = weights - part.astype(jnp.float32)
        parts.append(part)
    mixture = jnp.dot(parts[2], rows[...], preferred_element_type=jnp.float32)
    for part in (parts[1], parts[0]):
        mixture = mixture + jnp.dot(part, rows[...], preferred_element_type=jnp.float32)
    requests = out_ref.shape[1]
    for t in range(STEPS):
        out_ref[t] = mixture[t * requests : (t + 1) * requests].astype(jnp.bfloat16)


def collect(both, own, combine, sections, columns):
    features = both.shape[-1]
    requests = combine.shape[0] // STEPS
    in_vmem = pl.BlockSpec(memory_space=pltpu.VMEM)
    count = sections * columns
    return pl.pallas_call(
        functools.partial(collect_kernel, sections, columns),
        out_shape=jax.ShapeDtypeStruct((STEPS, requests, features), jnp.bfloat16),
        in_specs=[in_vmem] * 3,
        out_specs=in_vmem,
        scratch_shapes=[pltpu.VMEM(((count + columns) * CAP, features), jnp.bfloat16)]
        + exchange_scratch(sections, columns, count, features),
        compiler_params=pltpu.CompilerParams(collective_id=2, has_side_effects=True),
        name="collect",
    )(both, own, combine)


FIRST, AGAIN, OWN, CROSSED = 0, 1, 2, 3


def experts_kernel(
    both_ref,
    own_ref,
    gate_ref,
    up_ref,
    down_ref,
    both_out,
    own_out,
    gate,
    up,
    down,
    rows_0,
    rows_mid,
    rows_4,
    part_0,
    part_mid,
    part_4,
    other_0,
    other_mid,
    other_4,
    ring,
    crossed,
    hidden,
    load_sem,
    gather_send,
    gather_recv,
    share_send,
    share_recv,
    cross_send,
    cross_recv,
    pair_send,
    pair_recv,
    return_send,
    return_recv,
    reduce_send,
    reduce_recv,
):
    chunk = own_ref.shape[0]
    size = 4 * chunk
    features = own_ref.shape[1]
    wide = min(1024, features)
    narrow = min(512, features)
    section = lax.axis_index("sec")
    device = lax.axis_index("dev")
    column, z, core = device // LANE, (device % LANE) // 2, device % 2

    def at_z(where):
        return (section, column * LANE + ((where + RING) % RING) * 2 + core)

    sign = 1 - 2 * core
    onward = (at_z(z + sign), at_z(z - sign))
    back = (onward[1], onward[0])
    partner = (section, device + 1 - 2 * core)
    opposite = (1 - section, device)

    def remote(source, target, send_sem, recv_sem, where):
        return pltpu.make_async_remote_copy(
            src_ref=source,
            dst_ref=target,
            send_sem=send_sem,
            recv_sem=recv_sem,
            device_id=where,
            device_id_type=MESH,
        )

    loads = [
        pltpu.make_async_copy(own_ref, rows_0.at[pl.ds(OWN * chunk, chunk)], load_sem.at[0]),
        pltpu.make_async_copy(both_ref, rows_0.at[pl.ds(0, 2 * chunk)], load_sem.at[1]),
        pltpu.make_async_copy(gate_ref.at[0], gate, load_sem.at[2]),
        pltpu.make_async_copy(up_ref.at[0], up, load_sem.at[3]),
        pltpu.make_async_copy(down_ref.at[0], down, load_sem.at[4]),
    ]
    for load in loads:
        load.start()
    barrier = pltpu.get_barrier_semaphore()
    for where in onward + (partner, opposite):
        pl.semaphore_signal(barrier, inc=1, device_id=where, device_id_type=MESH)
    pl.semaphore_wait(barrier, 4)
    loads[0].wait()
    loads[1].wait()
    sends = []

    def start(copy):
        copy.start()
        sends.append(copy)

    def block_at(buffers, k, direction, c, of_partner=0):
        at = of_partner * size + c * chunk
        if k == 0:
            return buffers[0].at[pl.ds(at, chunk)]
        if k == 4:
            return buffers[2].at[pl.ds(at, chunk)]
        return buffers[1].at[k - 1, pl.ds(direction * 2 * size + at, chunk)]

    rows_at = functools.partial(block_at, (rows_0, rows_mid, rows_4))
    part_at = functools.partial(block_at, (part_0, part_mid, part_4))

    def gather(k, direction, c):
        return remote(
            rows_at(k - 1, direction, c),
            rows_at(k, direction, c),
            gather_send.at[k - 1, direction, c],
            gather_recv.at[k - 1, direction, c],
            onward[direction],
        )

    def share(k, direction, c):
        return remote(
            rows_at(k, direction, c),
            rows_at(k, direction, c, 1),
            share_send.at[k, direction, c],
            share_recv.at[k, direction, c],
            partner,
        )

    def cross(k, direction):
        return remote(
            rows_at(k, direction, OWN),
            rows_at(k, direction, CROSSED),
            cross_send.at[k, direction],
            cross_recv.at[k, direction],
            opposite,
        )

    def ringed(k):
        if k == 0:
            return []
        if k == 4:
            return [(1, OWN), (0, FIRST), (0, AGAIN)]
        return [(d, c) for c in (OWN, FIRST, AGAIN) for d in (0, 1)]

    def directions(k):
        return (0, 1) if 0 < k < 4 else (0,)

    def home(k, direction):
        return direction if 0 < k < 4 else 0

    def multiply(rows, part):
        count = rows.shape[0]

        x = rows[...]
        value = lax.dot_general(x, gate[...], CONTRACT_LAST, preferred_element_type=jnp.float32)
        value = value / (1.0 + jnp.exp(-value))
        value = value * lax.dot_general(
            x, up[...], CONTRACT_LAST, preferred_element_type=jnp.float32
        )
        hidden[pl.ds(0, count)] = value.astype(jnp.bfloat16)

        def output_step(i, carry):
            at = pl.ds(pl.multiple_of(i * wide, wide), wide)
            part[:, at] = jnp.dot(
                hidden[pl.ds(0, count)], down[:, at], preferred_element_type=jnp.float32
            ).astype(jnp.bfloat16)
            return carry

        lax.fori_loop(0, features // wide, output_step, 0)

    def pair(k, direction):
        if k == 0:
            source, target = part_0.at[pl.ds(size, size)], other_0
        elif k == 4:
            source, target = part_4.at[pl.ds(size, size)], other_4
        else:
            source = part_mid.at[k - 1, pl.ds(direction * 2 * size + size, size)]
            target = other_mid.at[k - 1, pl.ds(direction * size, size)]
        return remote(
            source, target, pair_send.at[k, direction], pair_recv.at[k, direction], partner
        )

    def other_at(k, direction, c):
        if k == 0:
            return other_0.at[pl.ds(c * chunk, chunk)]
        if k == 4:
            return other_4.at[pl.ds(c * chunk, chunk)]
        return other_mid.at[k - 1, pl.ds(direction * size + c * chunk, chunk)]

    def cross_back(k, direction):
        return remote(
            part_at(k, direction, CROSSED),
            crossed.at[k, direction],
            return_send.at[k, direction],
            return_recv.at[k, direction],
            opposite,
        )

    def ring_at(k, direction, c):
        return ring.at[k, direction, pl.ds(c * chunk, chunk)]

    def reduce(k, direction, c):
        return remote(
            part_at(k, direction, c),
            ring_at(k - 1, direction, c),
            reduce_send.at[k - 1, direction, c],
            reduce_recv.at[k - 1, direction, c],
            back[direction],
        )

    def add(target, sources):
        def step(i, carry):
            at = pl.ds(pl.multiple_of(i * narrow, narrow), narrow)
            total = sources[0][:, at].astype(jnp.float32)
            for source in sources[1:]:
                total = total + source[:, at].astype(jnp.float32)
            target[:, at] = total.astype(jnp.bfloat16)
            return carry

        lax.fori_loop(0, features // narrow, step, 0)

    def send_crossed_sums(k):
        for direction in directions(k):
            pair(k, direction).wait_recv()
            target = part_at(k, direction, CROSSED)
            add(target, [target, other_at(k, direction, CROSSED)])
            start(cross_back(k, direction))

    def send_sums(k, direction, c, from_ring=True):
        sources = [part_at(k, direction, c), other_at(k, direction, c)]
        if c == OWN:
            cross_back(k, home(k, direction)).wait_recv()
            sources.append(crossed.at[k, home(k, direction)])
        if from_ring:
            reduce(k + 1, direction, c).wait_recv()
            sources.append(ring_at(k, direction, c))
        add(sources[0], sources)
        start(reduce(k, direction, c))

    def take_in(k, arrivals):
        for direction, c in arrivals:
            gather(k, direction, c).wait_recv()
            if k < 3 or (k == 3 and (direction, c) in ringed(4)):
                start(gather(k + 1, direction, c))
            if c == OWN:
                start(cross(k, home(k, direction)))
            start(share(k, home(k, direction), c))

    def work_on(k):
        for direction in directions(k):
            cross(k, direction).wait_recv()
            start(share(k, direction, CROSSED))
        for direction in directions(k):
            for c in range(4):
                share(k, direction, c).wait_recv()
        if k == 0:
            multiply(rows_0, part_0)
        elif k == 4:
            multiply(rows_4, part_4)
        else:
            multiply(rows_mid.at[k - 1], part_mid.at[k - 1])
        for direction in directions(k):
            start(pair(k, direction))

    for c in (OWN, FIRST, AGAIN):
        for direction in range(2):
            start(gather(1, direction, c))
        if c == OWN:
            start(cross(0, 0))
        start(share(0, 0, c))

    take_in(1, ringed(1)[:2])
    for load in loads[2:]:
        load.wait()
    work_on(0)
    take_in(1, ringed(1)[2:])
    take_in(2, ringed(2)[:2])
    work_on(1)
    take_in(2, ringed(2)[2:])
    take_in(3, ringed(3)[:2])
    work_on(2)
    take_in(3, ringed(3)[2:])
    take_in(4, ringed(4)[:1])
    work_on(3)
    send_crossed_sums(3)
    take_in(4, ringed(4)[1:])
    for direction, c in ((1, FIRST), (1, AGAIN), (0, OWN)):
        send_sums(3, direction, c, from_ring=False)
    work_on(4)

    send_crossed_sums(4)
    send_sums(4, 0, FIRST, from_ring=False)
    send_sums(4, 0, AGAIN, from_ring=False)
    send_sums(4, 1, OWN, from_ring=False)
    send_crossed_sums(2)
    for c, direction in ((FIRST, 0), (AGAIN, 0), (OWN, 1)):
        send_sums(3, direction, c)
    send_crossed_sums(1)
    for k in (2, 1):
        for i in range(3):
            send_sums(k, 0, (OWN, FIRST, AGAIN)[i])
            send_sums(k, 1, (FIRST, AGAIN, OWN)[i])
        if k == 2:
            send_crossed_sums(0)
    for direction in range(2):
        for c in (FIRST, AGAIN, OWN):
            reduce(1, direction, c).wait_recv()
    cross_back(0, 0).wait_recv()
    own_rows = pl.ds(OWN * chunk, chunk)
    add(
        own_out,
        [
            part_0.at[own_rows],
            other_0.at[own_rows],
            crossed.at[0, 0],
            ring.at[0, 0, own_rows],
            ring.at[0, 1, own_rows],
        ],
    )
    both_rows = pl.ds(0, 2 * chunk)
    add(
        both_out,
        [
            part_0.at[both_rows],
            other_0.at[both_rows],
            ring.at[0, 0, both_rows],
            ring.at[0, 1, both_rows],
        ],
    )
    for copy in sends:
        copy.wait_send()


def run_experts(both, own, gate_weight, up_weight, down_weight):
    chunk, features = own.shape
    size = 4 * chunk
    units = gate_weight.shape[1]
    bf16 = jnp.bfloat16
    anywhere = pl.BlockSpec(memory_space=pl.ANY)
    in_vmem = pl.BlockSpec(memory_space=pltpu.VMEM)
    dma = pltpu.SemaphoreType.DMA
    return pl.pallas_call(
        experts_kernel,
        out_shape=(
            jax.ShapeDtypeStruct(both.shape, bf16),
            jax.ShapeDtypeStruct(own.shape, bf16),
        ),
        in_specs=[anywhere] * 5,
        out_specs=(in_vmem, in_vmem),
        scratch_shapes=[
            pltpu.VMEM((units, features), bf16),
            pltpu.VMEM((units, features), bf16),
            pltpu.VMEM((units, features), bf16),
            pltpu.VMEM((2 * size, features), bf16),
            pltpu.VMEM((3, 4 * size, features), bf16),
            pltpu.VMEM((2 * size, features), bf16),
            pltpu.VMEM((2 * size, features), bf16),
            pltpu.VMEM((3, 4 * size, features), bf16),
            pltpu.VMEM((2 * size, features), bf16),
            pltpu.VMEM((size, features), bf16),
            pltpu.VMEM((3, 2 * size, features), bf16),
            pltpu.VMEM((size, features), bf16),
            pltpu.VMEM((4, 2, 3 * chunk, features), bf16),
            pltpu.VMEM((5, 2, chunk, features), bf16),
            pltpu.VMEM((4 * size, units), bf16),
            dma((5,)),
            dma((4, 2, 3)),
            dma((4, 2, 3)),
            dma((5, 2, 4)),
            dma((5, 2, 4)),
            dma((5, 2)),
            dma((5, 2)),
            dma((5, 2)),
            dma((5, 2)),
            dma((5, 2)),
            dma((5, 2)),
            dma((4, 2, 3)),
            dma((4, 2, 3)),
        ],
        compiler_params=pltpu.CompilerParams(
            collective_id=1, has_side_effects=True, vmem_limit_bytes=60 * 1024 * 1024
        ),
        name="experts",
    )(both, own, gate_weight, up_weight, down_weight)


def body(
    sections,
    columns,
    hidden_in,
    queries,
    new_entries,
    request_cache_rows,
    lengths,
    expert_ids,
    route_weights,
    gate_weight,
    up_weight,
    down_weight,
):
    requests = hidden_in.shape[1]
    attended = attend(queries, new_entries, request_cache_rows, lengths)

    choices = expert_ids.reshape(STEPS, 2 * requests)
    same = choices[:, :, None] == choices[:, None, :]
    earlier = jnp.tril(jnp.ones((2 * requests, 2 * requests), jnp.bool_), -1)
    rank = jnp.sum((same & earlier[None]).astype(jnp.int32), axis=2)
    slot = jnp.arange(STEPS, dtype=jnp.int32)[:, None] * (E * CAP) + choices * CAP + rank
    slot = slot.reshape(STEPS * requests, 2)
    targets = jnp.arange(STEPS * E * CAP, dtype=jnp.int32)
    chosen = slot[:, :, None] == targets[None, None, :]
    selector = jnp.any(chosen, axis=1).astype(jnp.bfloat16).T
    combine = jnp.sum(
        chosen.astype(jnp.float32) * route_weights.reshape(STEPS * requests, 2)[:, :, None], axis=1
    )
    combine = jnp.concatenate([combine[:, : E * CAP]] * sections + [combine[:, E * CAP :]], axis=1)

    both, own = dispatch(attended, hidden_in, selector, sections, columns)
    both, own = run_experts(both, own, gate_weight, up_weight, down_weight)
    return attended, collect(both, own, combine, sections, columns)


def solution(mesh):
    sections, columns = mesh.shape["sec"], mesh.shape["dev"] // LANE
    placed = (
        P(None, ("sec", "dev"), None),
        P(None, ("sec", "dev"), None),
        P(None, ("sec", "dev"), None),
        P(("sec", "dev"), None, None),
        P(("sec", "dev")),
        P(None, ("sec", "dev"), None),
        P(None, ("sec", "dev"), None),
        P("sec", "dev", None),
        P("sec", "dev", None),
        P("sec", "dev", None),
    )
    return jax.shard_map(
        functools.partial(body, sections, columns),
        mesh=mesh,
        in_specs=placed,
        out_specs=(P(None, ("sec", "dev"), None), P(None, ("sec", "dev"), None)),
        check_vma=False,
    )
```

```python
import functools
import math

import jax
import jax.numpy as jnp
from jax import lax
from jax.experimental import pallas as pl
from jax.experimental.pallas import tpu as pltpu
from jax.sharding import PartitionSpec as P

QUERY_HEADS = 48
KEY_VALUE_HEADS = 8
HEAD_SIZE = 128
E = 8
LONGEST_LENGTH = 192
CAP = 2
STEPS = 2
GROUP = QUERY_HEADS // KEY_VALUE_HEADS
PADDED_GROUP = 8
RING = 8
LANE = 2 * RING
MESH = pl.DeviceIdType.MESH
CONTRACT_LAST = (((1,), (1,)), ((), ()))


def attend_kernel(lengths_ref, q_ref, fresh_ref, cache_ref, out_ref, cache, sem):
    requests = cache.shape[0]
    rows = STEPS * PADDED_GROUP
    key_width = KEY_VALUE_HEADS * HEAD_SIZE
    scale = 1.0 / math.sqrt(HEAD_SIZE)
    loads = [
        pltpu.make_async_copy(cache_ref.at[r], cache.at[r], sem.at[r]) for r in range(requests)
    ]
    for load in loads:
        load.start()
    every = KEY_VALUE_HEADS * rows
    place = lax.broadcasted_iota(jnp.int32, (every, LONGEST_LENGTH), 1)
    second = (lax.broadcasted_iota(jnp.int32, (every, 1), 0) // PADDED_GROUP) % STEPS == 1
    for r in range(requests):
        fresh_keys, fresh_values = [], []
        for t in range(STEPS):
            entry = fresh_ref[t, pl.ds(r, 1), :].astype(jnp.float32)
            fresh_keys.append(entry[:, :key_width])
            fresh_values.append(entry[:, key_width:])
        loads[r].wait()
        past, fresh = [], [[] for t in range(STEPS)]
        for head in range(KEY_VALUE_HEADS):
            lanes = slice(head * HEAD_SIZE, (head + 1) * HEAD_SIZE)
            q = q_ref[r, head]
            past.append(
                lax.dot_general(
                    q, cache[r, :, lanes], CONTRACT_LAST, preferred_element_type=jnp.float32
                )
            )
            wide = q.astype(jnp.float32)
            for t in range(STEPS):
                fresh[t].append(jnp.sum(wide * fresh_keys[t][:, lanes], axis=1, keepdims=True))
        past = jnp.concatenate(past, axis=0) * scale
        past = jnp.where(place < lengths_ref[r], past, -jnp.inf)
        fresh = [jnp.concatenate(part, axis=0) * scale for part in fresh]
        fresh[1] = jnp.where(second, fresh[1], -jnp.inf)
        top = jnp.maximum(jnp.max(past, axis=1, keepdims=True), jnp.maximum(fresh[0], fresh[1]))
        past = jnp.exp(past - top)
        fresh = [jnp.exp(part - top) for part in fresh]
        total = jnp.sum(past, axis=1, keepdims=True) + (fresh[0] + fresh[1])
        past = (past / total).astype(jnp.bfloat16)
        fresh = [(part / total).astype(jnp.bfloat16).astype(jnp.float32) for part in fresh]
        for head in range(KEY_VALUE_HEADS):
            lanes = slice(head * HEAD_SIZE, (head + 1) * HEAD_SIZE)
            values = slice(key_width + head * HEAD_SIZE, key_width + (head + 1) * HEAD_SIZE)
            here = slice(head * rows, (head + 1) * rows)
            mixed = jnp.dot(past[here], cache[r, :, values], preferred_element_type=jnp.float32)
            for t in range(STEPS):
                mixed = mixed + fresh[t][here] * fresh_values[t][:, lanes]
            out_ref[r, head] = mixed.astype(jnp.bfloat16)


def attend(queries, new_entries, request_cache_rows, lengths):
    requests = queries.shape[1]
    rows = STEPS * PADDED_GROUP
    q = queries.reshape(STEPS, requests, KEY_VALUE_HEADS, GROUP, HEAD_SIZE)
    q = jnp.pad(q, ((0, 0), (0, 0), (0, 0), (0, PADDED_GROUP - GROUP), (0, 0)))
    q = q.transpose(1, 2, 0, 3, 4).reshape(requests, KEY_VALUE_HEADS, rows, HEAD_SIZE)
    in_vmem = pl.BlockSpec(memory_space=pltpu.VMEM)
    out = pl.pallas_call(
        attend_kernel,
        out_shape=jax.ShapeDtypeStruct(q.shape, jnp.bfloat16),
        in_specs=[
            pl.BlockSpec(memory_space=pltpu.SMEM),
            in_vmem,
            in_vmem,
            pl.BlockSpec(memory_space=pl.ANY),
        ],
        out_specs=in_vmem,
        scratch_shapes=[
            pltpu.VMEM(request_cache_rows.shape, jnp.bfloat16),
            pltpu.SemaphoreType.DMA((requests,)),
        ],
        name="attend",
    )(lengths, q, new_entries, request_cache_rows)
    out = out.reshape(requests, KEY_VALUE_HEADS, STEPS, PADDED_GROUP, HEAD_SIZE)[:, :, :, :GROUP]
    return out.transpose(2, 0, 1, 3, 4).reshape(STEPS, requests, QUERY_HEADS * HEAD_SIZE)


FIRST, AGAIN, OWN, CROSSED = 0, 1, 2, 3


def experts_kernel(
    columns,
    attended_ref,
    hidden_ref,
    selector_ref,
    combine_ref,
    gate_ref,
    up_ref,
    down_ref,
    out_ref,
    gate,
    up,
    down,
    rows_0,
    rows_mid,
    rows_4,
    part_0,
    part_mid,
    part_4,
    other_0,
    other_mid,
    other_4,
    ring,
    crossed,
    hidden,
    slot_out,
    slot_in,
    sum_out,
    sum_in,
    load_sem,
    slot_send,
    slot_recv,
    sum_send,
    sum_recv,
    gather_send,
    gather_recv,
    share_send,
    share_recv,
    cross_send,
    cross_recv,
    pair_send,
    pair_recv,
    return_send,
    return_recv,
    reduce_send,
    reduce_recv,
):
    chunk = columns * CAP
    size = 4 * chunk
    features = hidden_ref.shape[-1]
    narrow = min(512, features)
    wide = min(1024, features)
    section = lax.axis_index("sec")
    device = lax.axis_index("dev")
    lane = device % LANE
    column, z, core = device // LANE, lane // 2, device % 2

    def at_z(where):
        return (section, column * LANE + ((where + RING) % RING) * 2 + core)

    sign = 1 - 2 * core
    onward = (at_z(z + sign), at_z(z - sign))
    back = (onward[1], onward[0])
    partner = (section, device + 1 - 2 * core)
    opposite = (1 - section, device)

    def remote(source, target, send_sem, recv_sem, where):
        return pltpu.make_async_remote_copy(
            src_ref=source,
            dst_ref=target,
            send_sem=send_sem,
            recv_sem=recv_sem,
            device_id=where,
            device_id_type=MESH,
        )

    loads = [
        pltpu.make_async_copy(gate_ref.at[0], gate, load_sem.at[0]),
        pltpu.make_async_copy(up_ref.at[0], up, load_sem.at[1]),
        pltpu.make_async_copy(down_ref.at[0], down, load_sem.at[2]),
    ]
    for load in loads:
        load.start()
    in_plane = [
        (where, ((column + offset) % columns) * LANE + lane)
        for where in (section, 1 - section)
        for offset in range(columns)
    ][1:]
    barrier = pltpu.get_barrier_semaphore()
    greeted = onward + (partner,) + tuple(in_plane)
    for where in greeted:
        pl.semaphore_signal(barrier, inc=1, device_id=where, device_id_type=MESH)
    sends = []

    def start(copy):
        copy.start()
        sends.append(copy)

    def exchange(c, source, target, send_sem, recv_sem, local_sem):
        there = 1 - section if c == AGAIN else section
        copies = []
        for offset in range(columns):
            peer = (column + offset) % columns
            if c != AGAIN and offset == 0:
                copy = pltpu.make_async_copy(source.at[peer], target.at[c, column], local_sem)
                copy.start()
                copies.append((copy, copy.wait))
                continue
            copy = remote(
                source.at[peer],
                target.at[c, column],
                send_sem.at[c, offset],
                recv_sem.at[c, offset],
                (there, peer * LANE + lane),
            )
            start(copy)
            copies.append((copy, copy.wait_recv))
        return [wait for copy, wait in copies]

    def block_at(buffers, k, direction, c, of_partner=0):
        at = of_partner * size + c * chunk
        if k == 0:
            return buffers[0].at[pl.ds(at, chunk)]
        if k == 4:
            return buffers[2].at[pl.ds(at, chunk)]
        return buffers[1].at[k - 1, pl.ds(direction * 2 * size + at, chunk)]

    rows_at = functools.partial(block_at, (rows_0, rows_mid, rows_4))
    part_at = functools.partial(block_at, (part_0, part_mid, part_4))

    def gather(k, direction, c):
        return remote(
            rows_at(k - 1, direction, c),
            rows_at(k, direction, c),
            gather_send.at[k - 1, direction, c],
            gather_recv.at[k - 1, direction, c],
            onward[direction],
        )

    def share(k, direction, c):
        return remote(
            rows_at(k, direction, c),
            rows_at(k, direction, c, 1),
            share_send.at[k, direction, c],
            share_recv.at[k, direction, c],
            partner,
        )

    def cross(k, direction):
        return remote(
            rows_at(k, direction, OWN),
            rows_at(k, direction, CROSSED),
            cross_send.at[k, direction],
            cross_recv.at[k, direction],
            opposite,
        )

    def ringed(k):
        if k == 0:
            return []
        if k == 4:
            return [(1, OWN), (0, FIRST), (0, AGAIN)]
        return [(d, c) for c in (OWN, FIRST, AGAIN) for d in (0, 1)]

    def directions(k):
        return (0, 1) if 0 < k < 4 else (0,)

    def home(k, direction):
        return direction if 0 < k < 4 else 0

    def multiply(rows, part):
        count = rows.shape[0]

        x = rows[...]
        value = lax.dot_general(x, gate[...], CONTRACT_LAST, preferred_element_type=jnp.float32)
        value = value / (1.0 + jnp.exp(-value))
        value = value * lax.dot_general(
            x, up[...], CONTRACT_LAST, preferred_element_type=jnp.float32
        )
        hidden[pl.ds(0, count)] = value.astype(jnp.bfloat16)

        def output_step(i, carry):
            at = pl.ds(pl.multiple_of(i * wide, wide), wide)
            part[:, at] = jnp.dot(
                hidden[pl.ds(0, count)], down[:, at], preferred_element_type=jnp.float32
            ).astype(jnp.bfloat16)
            return carry

        lax.fori_loop(0, features // wide, output_step, 0)

    def pair(k, direction):
        if k == 0:
            source, target = part_0.at[pl.ds(size, size)], other_0
        elif k == 4:
            source, target = part_4.at[pl.ds(size, size)], other_4
        else:
            source = part_mid.at[k - 1, pl.ds(direction * 2 * size + size, size)]
            target = other_mid.at[k - 1, pl.ds(direction * size, size)]
        return remote(
            source, target, pair_send.at[k, direction], pair_recv.at[k, direction], partner
        )

    def other_at(k, direction, c):
        if k == 0:
            return other_0.at[pl.ds(c * chunk, chunk)]
        if k == 4:
            return other_4.at[pl.ds(c * chunk, chunk)]
        return other_mid.at[k - 1, pl.ds(direction * size + c * chunk, chunk)]

    def cross_back(k, direction):
        return remote(
            part_at(k, direction, CROSSED),
            crossed.at[k, direction],
            return_send.at[k, direction],
            return_recv.at[k, direction],
            opposite,
        )

    def ring_at(k, direction, c):
        return ring.at[k, direction, pl.ds(c * chunk, chunk)]

    def reduce(k, direction, c):
        return remote(
            part_at(k, direction, c),
            ring_at(k - 1, direction, c),
            reduce_send.at[k - 1, direction, c],
            reduce_recv.at[k - 1, direction, c],
            back[direction],
        )

    def add(target, sources):
        def step(i, carry):
            at = pl.ds(pl.multiple_of(i * narrow, narrow), narrow)
            total = sources[0][:, at].astype(jnp.float32)
            for source in sources[1:]:
                total = total + source[:, at].astype(jnp.float32)
            target[:, at] = total.astype(jnp.bfloat16)
            return carry

        lax.fori_loop(0, features // narrow, step, 0)

    def send_crossed_sums(k):
        for direction in directions(k):
            pair(k, direction).wait_recv()
            target = part_at(k, direction, CROSSED)
            add(target, [target, other_at(k, direction, CROSSED)])
            start(cross_back(k, direction))

    def send_sums(k, direction, c, from_ring=True):
        sources = [part_at(k, direction, c), other_at(k, direction, c)]
        if c == OWN:
            cross_back(k, home(k, direction)).wait_recv()
            sources.append(crossed.at[k, home(k, direction)])
        if from_ring:
            reduce(k + 1, direction, c).wait_recv()
            sources.append(ring_at(k, direction, c))
        add(sources[0], sources)
        start(reduce(k, direction, c))

    def take_in(k, arrivals):
        for direction, c in arrivals:
            gather(k, direction, c).wait_recv()
            if k < 3 or (k == 3 and (direction, c) in ringed(4)):
                start(gather(k + 1, direction, c))
            if c == OWN:
                start(cross(k, home(k, direction)))
            start(share(k, home(k, direction), c))

    def work_on(k):
        for direction in directions(k):
            cross(k, direction).wait_recv()
            start(share(k, direction, CROSSED))
        for direction in directions(k):
            for c in range(4):
                share(k, direction, c).wait_recv()
        if k == 0:
            multiply(rows_0, part_0)
        elif k == 4:
            multiply(rows_4, part_4)
        else:
            multiply(rows_mid.at[k - 1], part_mid.at[k - 1])
        for direction in directions(k):
            start(pair(k, direction))

    residual_sum = jnp.concatenate(
        [
            hidden_ref[t].astype(jnp.float32) + attended_ref[t].astype(jnp.float32)
            for t in range(STEPS)
        ],
        axis=0,
    )
    mean_square = jnp.mean(residual_sum * residual_sum, axis=-1, keepdims=True)
    normed = (residual_sum * lax.rsqrt(mean_square + 1e-05)).astype(jnp.bfloat16)
    slots = jnp.dot(selector_ref[...], normed, preferred_element_type=jnp.float32)
    slots = slots.astype(jnp.bfloat16)
    for t in range(STEPS):
        for e in range(columns):
            at = CAP * (t * columns + e)
            slot_out[t, e] = slots[at : at + CAP]
    pl.semaphore_wait(barrier, len(greeted))
    arrivals = {
        c: exchange(
            c, slot_out.at[1 if c == OWN else 0], slot_in, slot_send, slot_recv, load_sem.at[3 + c]
        )
        for c in (OWN, FIRST, AGAIN)
    }

    for c in (OWN, FIRST, AGAIN):
        for wait in arrivals[c]:
            wait()
        for j in range(columns):
            rows_0[pl.ds(c * chunk + CAP * j, CAP)] = slot_in[c, j]
        for direction in range(2):
            start(gather(1, direction, c))
        if c == OWN:
            start(cross(0, 0))
        start(share(0, 0, c))

    take_in(1, ringed(1)[:2])
    for load in loads:
        load.wait()
    work_on(0)
    take_in(1, ringed(1)[2:])
    take_in(2, ringed(2)[:2])
    work_on(1)
    take_in(2, ringed(2)[2:])
    take_in(3, ringed(3)[:2])
    work_on(2)
    take_in(3, ringed(3)[2:])
    take_in(4, ringed(4)[:1])
    work_on(3)
    send_crossed_sums(3)
    take_in(4, ringed(4)[1:])
    for direction, c in ((1, FIRST), (1, AGAIN), (0, OWN)):
        send_sums(3, direction, c, from_ring=False)
    work_on(4)

    send_crossed_sums(4)
    send_sums(4, 0, FIRST, from_ring=False)
    send_sums(4, 0, AGAIN, from_ring=False)
    send_sums(4, 1, OWN, from_ring=False)
    send_crossed_sums(2)
    for c, direction in ((FIRST, 0), (AGAIN, 0), (OWN, 1)):
        send_sums(3, direction, c)
    send_crossed_sums(1)
    for k in (2, 1):
        for i in range(3):
            send_sums(k, 0, (OWN, FIRST, AGAIN)[i])
            send_sums(k, 1, (FIRST, AGAIN, OWN)[i])
        if k == 2:
            send_crossed_sums(0)
    arrivals = []
    for c in (FIRST, AGAIN, OWN):
        at = pl.ds(c * chunk, chunk)
        sources = [part_0.at[at], other_0.at[at]]
        if c == OWN:
            cross_back(0, 0).wait_recv()
            sources.append(crossed.at[0, 0])
        for direction in range(2):
            reduce(1, direction, c).wait_recv()
            sources.append(ring_at(0, direction, c))
        add(part_0.at[at], sources)
        for j in range(columns):
            sum_out[c, j] = part_0[pl.ds(c * chunk + CAP * j, CAP)]
        arrivals += exchange(c, sum_out.at[c], sum_in, sum_send, sum_recv, load_sem.at[6 + c])
    for wait in arrivals:
        wait()
    for copy in sends:
        copy.wait_send()
    for c in (FIRST, AGAIN, OWN):
        for j in range(columns):
            part_4[pl.ds(c * chunk + CAP * j, CAP)] = sum_in[c, j]

    weights = combine_ref[...]
    parts = []
    for _ in range(3):
        part = weights.astype(jnp.bfloat16)
        weights = weights - part.astype(jnp.float32)
        parts.append(part)

    def mix_step(i, carry):
        at = pl.ds(pl.multiple_of(i * wide, wide), wide)
        rows = part_4[pl.ds(0, 3 * chunk), at]
        mixture = jnp.dot(parts[2], rows, preferred_element_type=jnp.float32)
        for part in (parts[1], parts[0]):
            mixture = mixture + jnp.dot(part, rows, preferred_element_type=jnp.float32)
        out_ref[:, at] = mixture.astype(jnp.bfloat16)
        return carry

    lax.fori_loop(0, features // wide, mix_step, 0)


def run_experts(
    columns, attended, hidden_in, selector, combine, gate_weight, up_weight, down_weight
):
    features = hidden_in.shape[-1]
    chunk = columns * CAP
    size = 4 * chunk
    units = gate_weight.shape[1]
    bf16 = jnp.bfloat16
    anywhere = pl.BlockSpec(memory_space=pl.ANY)
    in_vmem = pl.BlockSpec(memory_space=pltpu.VMEM)
    dma = pltpu.SemaphoreType.DMA
    return pl.pallas_call(
        functools.partial(experts_kernel, columns),
        out_shape=jax.ShapeDtypeStruct((combine.shape[0], features), bf16),
        in_specs=[in_vmem] * 4 + [anywhere] * 3,
        out_specs=in_vmem,
        scratch_shapes=[
            pltpu.VMEM((units, features), bf16),
            pltpu.VMEM((units, features), bf16),
            pltpu.VMEM((units, features), bf16),
            pltpu.VMEM((2 * size, features), bf16),
            pltpu.VMEM((3, 4 * size, features), bf16),
            pltpu.VMEM((2 * size, features), bf16),
            pltpu.VMEM((2 * size, features), bf16),
            pltpu.VMEM((3, 4 * size, features), bf16),
            pltpu.VMEM((2 * size, features), bf16),
            pltpu.VMEM((size, features), bf16),
            pltpu.VMEM((3, 2 * size, features), bf16),
            pltpu.VMEM((size, features), bf16),
            pltpu.VMEM((4, 2, 3 * chunk, features), bf16),
            pltpu.VMEM((5, 2, chunk, features), bf16),
            pltpu.VMEM((4 * size, units), bf16),
            pltpu.VMEM((STEPS, columns, CAP, features), bf16),
            pltpu.VMEM((3, columns, CAP, features), bf16),
            pltpu.VMEM((3, columns, CAP, features), bf16),
            pltpu.VMEM((3, columns, CAP, features), bf16),
            dma((9,)),
            dma((3, columns)),
            dma((3, columns)),
            dma((3, columns)),
            dma((3, columns)),
            dma((4, 2, 3)),
            dma((4, 2, 3)),
            dma((5, 2, 4)),
            dma((5, 2, 4)),
            dma((5, 2)),
            dma((5, 2)),
            dma((5, 2)),
            dma((5, 2)),
            dma((5, 2)),
            dma((5, 2)),
            dma((4, 2, 3)),
            dma((4, 2, 3)),
        ],
        compiler_params=pltpu.CompilerParams(
            collective_id=0, has_side_effects=True, vmem_limit_bytes=60 * 1024 * 1024
        ),
        name="experts",
    )(attended, hidden_in, selector, combine, gate_weight, up_weight, down_weight)


def body(
    sections,
    columns,
    hidden_in,
    queries,
    new_entries,
    request_cache_rows,
    lengths,
    expert_ids,
    route_weights,
    gate_weight,
    up_weight,
    down_weight,
):
    requests = hidden_in.shape[1]
    attended = attend(queries, new_entries, request_cache_rows, lengths)

    choices = expert_ids.reshape(STEPS, 2 * requests)
    same = choices[:, :, None] == choices[:, None, :]
    earlier = jnp.tril(jnp.ones((2 * requests, 2 * requests), jnp.bool_), -1)
    rank = jnp.sum((same & earlier[None]).astype(jnp.int32), axis=2)
    slot = jnp.arange(STEPS, dtype=jnp.int32)[:, None] * (E * CAP) + choices * CAP + rank
    slot = slot.reshape(STEPS * requests, 2)
    targets = jnp.arange(STEPS * E * CAP, dtype=jnp.int32)
    chosen = slot[:, :, None] == targets[None, None, :]
    selector = jnp.any(chosen, axis=1).astype(jnp.bfloat16).T
    combine = jnp.sum(
        chosen.astype(jnp.float32) * route_weights.reshape(STEPS * requests, 2)[:, :, None], axis=1
    )
    combine = jnp.concatenate([combine[:, : E * CAP]] * sections + [combine[:, E * CAP :]], axis=1)

    mixture = run_experts(
        columns, attended, hidden_in, selector, combine, gate_weight, up_weight, down_weight
    )
    return attended, mixture.reshape(hidden_in.shape)


def solution(mesh):
    sections, columns = mesh.shape["sec"], mesh.shape["dev"] // LANE
    placed = (
        P(None, ("sec", "dev"), None),
        P(None, ("sec", "dev"), None),
        P(None, ("sec", "dev"), None),
        P(("sec", "dev"), None, None),
        P(("sec", "dev")),
        P(None, ("sec", "dev"), None),
        P(None, ("sec", "dev"), None),
        P("sec", "dev", None),
        P("sec", "dev", None),
        P("sec", "dev", None),
    )
    return jax.shard_map(
        functools.partial(body, sections, columns),
        mesh=mesh,
        in_specs=placed,
        out_specs=(P(None, ("sec", "dev"), None), P(None, ("sec", "dev"), None)),
        check_vma=False,
    )
```

```python
import functools
import math

import jax
import jax.numpy as jnp
from jax import lax
from jax.experimental import pallas as pl
from jax.experimental.pallas import tpu as pltpu
from jax.sharding import PartitionSpec as P

QUERY_HEADS = 48
KEY_VALUE_HEADS = 8
HEAD_SIZE = 128
E = 8
LONGEST_LENGTH = 192
CAP = 2
STEPS = 2
GROUP = QUERY_HEADS // KEY_VALUE_HEADS
PADDED_GROUP = 8
RING = 8
LANE = 2 * RING
MESH = pl.DeviceIdType.MESH
CONTRACT_LAST = (((1,), (1,)), ((), ()))


def attend_kernel(
    lengths_ref,
    experts_ref,
    weights_ref,
    q_ref,
    fresh_ref,
    cache_ref,
    out_ref,
    selector_ref,
    combine_ref,
    cache,
    q_rows,
    out_rows,
    sem,
):
    requests = cache.shape[0]
    rows = STEPS * PADDED_GROUP
    key_width = KEY_VALUE_HEADS * HEAD_SIZE
    scale = 1.0 / math.sqrt(HEAD_SIZE)
    loads = [
        pltpu.make_async_copy(cache_ref.at[r], cache.at[r], sem.at[r]) for r in range(requests)
    ]
    for load in loads:
        load.start()

    def head_lanes(head, i):
        return pl.ds((head * GROUP + i) * HEAD_SIZE, HEAD_SIZE)

    q_rows[...] = jnp.zeros_like(q_rows)
    for head in range(KEY_VALUE_HEADS):
        for t in range(STEPS):
            for i in range(GROUP):
                at = pl.ds((t * PADDED_GROUP + i) * requests, requests)
                q_rows[head, at] = q_ref[t, :, head_lanes(head, i)].astype(jnp.float32)

    slots, tokens = selector_ref.shape
    slot_at = lax.broadcasted_iota(jnp.int32, (slots, tokens), 0)
    token_at = lax.broadcasted_iota(jnp.int32, (slots, tokens), 1)
    row_at = lax.broadcasted_iota(jnp.int32, combine_ref.shape, 0)
    column_at = lax.broadcasted_iota(jnp.int32, combine_ref.shape, 1)
    selector = jnp.zeros((slots, tokens), jnp.float32)
    combine = jnp.zeros(combine_ref.shape, jnp.float32)
    for t in range(STEPS):
        named = []
        for r in range(requests):
            token = t * requests + r
            for j in range(2):
                expert = experts_ref[t, j, r]
                rank = jnp.int32(0)
                for earlier in named:
                    rank = rank + (earlier == expert).astype(jnp.int32)
                named.append(expert)
                slot = expert * CAP + rank
                selector = jnp.where(
                    (slot_at == slot + t * E * CAP) & (token_at == token), 1.0, selector
                )
                if t == 0:
                    here = (column_at == slot) | (column_at == slot + E * CAP)
                else:
                    here = column_at == slot + 2 * E * CAP
                combine = jnp.where(here & (row_at == token), weights_ref[t, j, r], combine)
    selector_ref[...] = selector.astype(jnp.bfloat16)
    combine_ref[...] = combine

    every = KEY_VALUE_HEADS * rows
    place = lax.broadcasted_iota(jnp.int32, (every, LONGEST_LENGTH), 1)
    second = (lax.broadcasted_iota(jnp.int32, (every, 1), 0) // PADDED_GROUP) % STEPS == 1
    for r in range(requests):
        of_request = pl.ds(r, rows, stride=requests)
        fresh_keys, fresh_values = [], []
        for t in range(STEPS):
            entry = fresh_ref[t, pl.ds(r, 1), :].astype(jnp.float32)
            fresh_keys.append(entry[:, :key_width])
            fresh_values.append(entry[:, key_width:])
        loads[r].wait()
        past, fresh = [], [[] for t in range(STEPS)]
        for head in range(KEY_VALUE_HEADS):
            lanes = slice(head * HEAD_SIZE, (head + 1) * HEAD_SIZE)
            wide = q_rows[head, of_request, :]
            past.append(
                lax.dot_general(
                    wide.astype(jnp.bfloat16),
                    cache[r, :, lanes],
                    CONTRACT_LAST,
                    preferred_element_type=jnp.float32,
                )
            )
            for t in range(STEPS):
                fresh[t].append(jnp.sum(wide * fresh_keys[t][:, lanes], axis=1, keepdims=True))
        past = jnp.concatenate(past, axis=0) * scale
        past = jnp.where(place < lengths_ref[r], past, -jnp.inf)
        fresh = [jnp.concatenate(part, axis=0) * scale for part in fresh]
        fresh[1] = jnp.where(second, fresh[1], -jnp.inf)
        top = jnp.maximum(jnp.max(past, axis=1, keepdims=True), jnp.maximum(fresh[0], fresh[1]))
        past = jnp.exp(past - top)
        fresh = [jnp.exp(part - top) for part in fresh]
        total = jnp.sum(past, axis=1, keepdims=True) + (fresh[0] + fresh[1])
        past = (past / total).astype(jnp.bfloat16)
        fresh = [(part / total).astype(jnp.bfloat16).astype(jnp.float32) for part in fresh]
        for head in range(KEY_VALUE_HEADS):
            lanes = slice(head * HEAD_SIZE, (head + 1) * HEAD_SIZE)
            values = slice(key_width + head * HEAD_SIZE, key_width + (head + 1) * HEAD_SIZE)
            here = slice(head * rows, (head + 1) * rows)
            mixed = jnp.dot(past[here], cache[r, :, values], preferred_element_type=jnp.float32)
            for t in range(STEPS):
                mixed = mixed + fresh[t][here] * fresh_values[t][:, lanes]
            out_rows[head, of_request, :] = mixed
    for head in range(KEY_VALUE_HEADS):
        for t in range(STEPS):
            for i in range(GROUP):
                at = pl.ds((t * PADDED_GROUP + i) * requests, requests)
                out_ref[t, :, head_lanes(head, i)] = out_rows[head, at].astype(jnp.bfloat16)


def attend(queries, new_entries, request_cache_rows, lengths, expert_ids, route_weights):
    steps, requests, features = queries.shape
    rows = STEPS * PADDED_GROUP * requests
    in_vmem = pl.BlockSpec(memory_space=pltpu.VMEM)
    in_smem = pl.BlockSpec(memory_space=pltpu.SMEM)
    return pl.pallas_call(
        attend_kernel,
        out_shape=(
            jax.ShapeDtypeStruct(queries.shape, jnp.bfloat16),
            jax.ShapeDtypeStruct((STEPS * E * CAP, STEPS * requests), jnp.bfloat16),
            jax.ShapeDtypeStruct((STEPS * requests, 3 * E * CAP), jnp.float32),
        ),
        in_specs=[in_smem] * 3 + [in_vmem] * 2 + [pl.BlockSpec(memory_space=pl.ANY)],
        out_specs=(in_vmem,) * 3,
        scratch_shapes=[
            pltpu.VMEM(request_cache_rows.shape, jnp.bfloat16),
            pltpu.VMEM((KEY_VALUE_HEADS, rows, HEAD_SIZE), jnp.float32),
            pltpu.VMEM((KEY_VALUE_HEADS, rows, HEAD_SIZE), jnp.float32),
            pltpu.SemaphoreType.DMA((requests,)),
        ],
        name="attend",
    )(
        lengths,
        expert_ids.transpose(0, 2, 1),
        route_weights.transpose(0, 2, 1),
        queries,
        new_entries,
        request_cache_rows,
    )


FIRST, AGAIN, OWN, CROSSED = 0, 1, 2, 3


def experts_kernel(
    columns,
    attended_ref,
    hidden_ref,
    selector_ref,
    combine_ref,
    gate_ref,
    up_ref,
    down_ref,
    out_ref,
    gate,
    up,
    down,
    rows_0,
    rows_mid,
    rows_4,
    part_0,
    part_mid,
    part_4,
    other_0,
    other_mid,
    other_4,
    ring,
    crossed,
    hidden,
    slot_out,
    slot_in,
    sum_out,
    sum_in,
    load_sem,
    slot_send,
    slot_recv,
    sum_send,
    sum_recv,
    gather_send,
    gather_recv,
    share_send,
    share_recv,
    cross_send,
    cross_recv,
    pair_send,
    pair_recv,
    return_send,
    return_recv,
    reduce_send,
    reduce_recv,
):
    chunk = columns * CAP
    size = 4 * chunk
    features = hidden_ref.shape[-1]
    narrow = min(512, features)
    wide = min(1024, features)
    section = lax.axis_index("sec")
    device = lax.axis_index("dev")
    lane = device % LANE
    column, z, core = device // LANE, lane // 2, device % 2

    def at_z(where):
        return (section, column * LANE + ((where + RING) % RING) * 2 + core)

    sign = 1 - 2 * core
    onward = (at_z(z + sign), at_z(z - sign))
    back = (onward[1], onward[0])
    partner = (section, device + 1 - 2 * core)
    opposite = (1 - section, device)

    def remote(source, target, send_sem, recv_sem, where):
        return pltpu.make_async_remote_copy(
            src_ref=source,
            dst_ref=target,
            send_sem=send_sem,
            recv_sem=recv_sem,
            device_id=where,
            device_id_type=MESH,
        )

    loads = [
        pltpu.make_async_copy(gate_ref.at[0], gate, load_sem.at[0]),
        pltpu.make_async_copy(up_ref.at[0], up, load_sem.at[1]),
        pltpu.make_async_copy(down_ref.at[0], down, load_sem.at[2]),
    ]
    for load in loads:
        load.start()
    in_plane = [
        (where, ((column + offset) % columns) * LANE + lane)
        for where in (section, 1 - section)
        for offset in range(columns)
    ][1:]
    barrier = pltpu.get_barrier_semaphore()
    greeted = onward + (partner,) + tuple(in_plane)
    for where in greeted:
        pl.semaphore_signal(barrier, inc=1, device_id=where, device_id_type=MESH)
    sends = []

    def start(copy):
        copy.start()
        sends.append(copy)

    def exchange(c, source, target, send_sem, recv_sem, local_sem):
        there = 1 - section if c == AGAIN else section
        copies = []
        for offset in range(columns):
            peer = (column + offset) % columns
            if c != AGAIN and offset == 0:
                copy = pltpu.make_async_copy(source.at[peer], target.at[c, column], local_sem)
                copy.start()
                copies.append((copy, copy.wait))
                continue
            copy = remote(
                source.at[peer],
                target.at[c, column],
                send_sem.at[c, offset],
                recv_sem.at[c, offset],
                (there, peer * LANE + lane),
            )
            start(copy)
            copies.append((copy, copy.wait_recv))
        return [wait for copy, wait in copies]

    def block_at(buffers, k, direction, c, of_partner=0):
        at = of_partner * size + c * chunk
        if k == 0:
            return buffers[0].at[pl.ds(at, chunk)]
        if k == 4:
            return buffers[2].at[pl.ds(at, chunk)]
        return buffers[1].at[k - 1, pl.ds(direction * 2 * size + at, chunk)]

    rows_at = functools.partial(block_at, (rows_0, rows_mid, rows_4))
    part_at = functools.partial(block_at, (part_0, part_mid, part_4))

    def gather(k, direction, c):
        return remote(
            rows_at(k - 1, direction, c),
            rows_at(k, direction, c),
            gather_send.at[k - 1, direction, c],
            gather_recv.at[k - 1, direction, c],
            onward[direction],
        )

    def share(k, direction, c):
        return remote(
            rows_at(k, direction, c),
            rows_at(k, direction, c, 1),
            share_send.at[k, direction, c],
            share_recv.at[k, direction, c],
            partner,
        )

    def cross(k, direction):
        return remote(
            rows_at(k, direction, OWN),
            rows_at(k, direction, CROSSED),
            cross_send.at[k, direction],
            cross_recv.at[k, direction],
            opposite,
        )

    def ringed(k):
        if k == 0:
            return []
        if k == 4:
            return [(1, OWN), (0, FIRST), (0, AGAIN)]
        return [(d, c) for c in (OWN, FIRST, AGAIN) for d in (0, 1)]

    def directions(k):
        return (0, 1) if 0 < k < 4 else (0,)

    def home(k, direction):
        return direction if 0 < k < 4 else 0

    def multiply(rows, part):
        count = rows.shape[0]

        x = rows[...]
        value = lax.dot_general(x, gate[...], CONTRACT_LAST, preferred_element_type=jnp.float32)
        value = value / (1.0 + jnp.exp(-value))
        value = value * lax.dot_general(
            x, up[...], CONTRACT_LAST, preferred_element_type=jnp.float32
        )
        hidden[pl.ds(0, count)] = value.astype(jnp.bfloat16)

        def output_step(i, carry):
            at = pl.ds(pl.multiple_of(i * wide, wide), wide)
            part[:, at] = jnp.dot(
                hidden[pl.ds(0, count)], down[:, at], preferred_element_type=jnp.float32
            ).astype(jnp.bfloat16)
            return carry

        lax.fori_loop(0, features // wide, output_step, 0)

    def pair(k, direction):
        if k == 0:
            source, target = part_0.at[pl.ds(size, size)], other_0
        elif k == 4:
            source, target = part_4.at[pl.ds(size, size)], other_4
        else:
            source = part_mid.at[k - 1, pl.ds(direction * 2 * size + size, size)]
            target = other_mid.at[k - 1, pl.ds(direction * size, size)]
        return remote(
            source, target, pair_send.at[k, direction], pair_recv.at[k, direction], partner
        )

    def other_at(k, direction, c):
        if k == 0:
            return other_0.at[pl.ds(c * chunk, chunk)]
        if k == 4:
            return other_4.at[pl.ds(c * chunk, chunk)]
        return other_mid.at[k - 1, pl.ds(direction * size + c * chunk, chunk)]

    def cross_back(k, direction):
        return remote(
            part_at(k, direction, CROSSED),
            crossed.at[k, direction],
            return_send.at[k, direction],
            return_recv.at[k, direction],
            opposite,
        )

    def ring_at(k, direction, c):
        return ring.at[k, direction, pl.ds(c * chunk, chunk)]

    def reduce(k, direction, c):
        return remote(
            part_at(k, direction, c),
            ring_at(k - 1, direction, c),
            reduce_send.at[k - 1, direction, c],
            reduce_recv.at[k - 1, direction, c],
            back[direction],
        )

    def add(target, sources):
        def step(i, carry):
            at = pl.ds(pl.multiple_of(i * narrow, narrow), narrow)
            total = sources[0][:, at].astype(jnp.float32)
            for source in sources[1:]:
                total = total + source[:, at].astype(jnp.float32)
            target[:, at] = total.astype(jnp.bfloat16)
            return carry

        lax.fori_loop(0, features // narrow, step, 0)

    def send_crossed_sums(k):
        for direction in directions(k):
            pair(k, direction).wait_recv()
            target = part_at(k, direction, CROSSED)
            add(target, [target, other_at(k, direction, CROSSED)])
            start(cross_back(k, direction))

    def send_sums(k, direction, c, from_ring=True):
        sources = [part_at(k, direction, c), other_at(k, direction, c)]
        if c == OWN:
            cross_back(k, home(k, direction)).wait_recv()
            sources.append(crossed.at[k, home(k, direction)])
        if from_ring:
            reduce(k + 1, direction, c).wait_recv()
            sources.append(ring_at(k, direction, c))
        add(sources[0], sources)
        start(reduce(k, direction, c))

    def take_in(k, arrivals):
        for direction, c in arrivals:
            gather(k, direction, c).wait_recv()
            if k < 3 or (k == 3 and (direction, c) in ringed(4)):
                start(gather(k + 1, direction, c))
            if c == OWN:
                start(cross(k, home(k, direction)))
            start(share(k, home(k, direction), c))

    def work_on(k):
        for direction in directions(k):
            cross(k, direction).wait_recv()
            start(share(k, direction, CROSSED))
        for direction in directions(k):
            for c in range(4):
                share(k, direction, c).wait_recv()
        if k == 0:
            multiply(rows_0, part_0)
        elif k == 4:
            multiply(rows_4, part_4)
        else:
            multiply(rows_mid.at[k - 1], part_mid.at[k - 1])
        for direction in directions(k):
            start(pair(k, direction))

    residual_sum = jnp.concatenate(
        [
            hidden_ref[t].astype(jnp.float32) + attended_ref[t].astype(jnp.float32)
            for t in range(STEPS)
        ],
        axis=0,
    )
    mean_square = jnp.mean(residual_sum * residual_sum, axis=-1, keepdims=True)
    normed = (residual_sum * lax.rsqrt(mean_square + 1e-05)).astype(jnp.bfloat16)
    slots = jnp.dot(selector_ref[...], normed, preferred_element_type=jnp.float32)
    slots = slots.astype(jnp.bfloat16)
    for t in range(STEPS):
        for e in range(columns):
            at = CAP * (t * columns + e)
            slot_out[t, e] = slots[at : at + CAP]
    pl.semaphore_wait(barrier, len(greeted))
    arrivals = {
        c: exchange(
            c, slot_out.at[1 if c == OWN else 0], slot_in, slot_send, slot_recv, load_sem.at[3 + c]
        )
        for c in (OWN, FIRST, AGAIN)
    }

    for c in (OWN, FIRST, AGAIN):
        for wait in arrivals[c]:
            wait()
        for j in range(columns):
            rows_0[pl.ds(c * chunk + CAP * j, CAP)] = slot_in[c, j]
        for direction in range(2):
            start(gather(1, direction, c))
        if c == OWN:
            start(cross(0, 0))
        start(share(0, 0, c))

    take_in(1, ringed(1)[:2])
    for load in loads:
        load.wait()
    work_on(0)
    take_in(1, ringed(1)[2:])
    take_in(2, ringed(2)[:2])
    work_on(1)
    take_in(2, ringed(2)[2:])
    take_in(3, ringed(3)[:2])
    work_on(2)
    take_in(3, ringed(3)[2:])
    take_in(4, ringed(4)[:1])
    work_on(3)
    send_crossed_sums(3)
    take_in(4, ringed(4)[1:])
    for direction, c in ((1, FIRST), (1, AGAIN), (0, OWN)):
        send_sums(3, direction, c, from_ring=False)
    work_on(4)

    send_crossed_sums(4)
    send_sums(4, 0, FIRST, from_ring=False)
    send_sums(4, 0, AGAIN, from_ring=False)
    send_sums(4, 1, OWN, from_ring=False)
    send_crossed_sums(2)
    for c, direction in ((FIRST, 0), (AGAIN, 0), (OWN, 1)):
        send_sums(3, direction, c)
    send_crossed_sums(1)
    for k in (2, 1):
        for i in range(3):
            send_sums(k, 0, (OWN, FIRST, AGAIN)[i])
            send_sums(k, 1, (FIRST, AGAIN, OWN)[i])
        if k == 2:
            send_crossed_sums(0)
    arrivals = []
    for c in (FIRST, AGAIN, OWN):
        at = pl.ds(c * chunk, chunk)
        sources = [part_0.at[at], other_0.at[at]]
        if c == OWN:
            cross_back(0, 0).wait_recv()
            sources.append(crossed.at[0, 0])
        for direction in range(2):
            reduce(1, direction, c).wait_recv()
            sources.append(ring_at(0, direction, c))
        add(part_0.at[at], sources)
        for j in range(columns):
            sum_out[c, j] = part_0[pl.ds(c * chunk + CAP * j, CAP)]
        arrivals += exchange(c, sum_out.at[c], sum_in, sum_send, sum_recv, load_sem.at[6 + c])
    for wait in arrivals:
        wait()
    for copy in sends:
        copy.wait_send()
    for c in (FIRST, AGAIN, OWN):
        for j in range(columns):
            part_4[pl.ds(c * chunk + CAP * j, CAP)] = sum_in[c, j]

    weights = combine_ref[...]
    parts = []
    for _ in range(3):
        part = weights.astype(jnp.bfloat16)
        weights = weights - part.astype(jnp.float32)
        parts.append(part)

    def mix_step(i, carry):
        at = pl.ds(pl.multiple_of(i * wide, wide), wide)
        rows = part_4[pl.ds(0, 3 * chunk), at]
        mixture = jnp.dot(parts[2], rows, preferred_element_type=jnp.float32)
        for part in (parts[1], parts[0]):
            mixture = mixture + jnp.dot(part, rows, preferred_element_type=jnp.float32)
        out_ref[:, at] = mixture.astype(jnp.bfloat16)
        return carry

    lax.fori_loop(0, features // wide, mix_step, 0)


def run_experts(
    columns, attended, hidden_in, selector, combine, gate_weight, up_weight, down_weight
):
    features = hidden_in.shape[-1]
    chunk = columns * CAP
    size = 4 * chunk
    units = gate_weight.shape[1]
    bf16 = jnp.bfloat16
    anywhere = pl.BlockSpec(memory_space=pl.ANY)
    in_vmem = pl.BlockSpec(memory_space=pltpu.VMEM)
    dma = pltpu.SemaphoreType.DMA
    return pl.pallas_call(
        functools.partial(experts_kernel, columns),
        out_shape=jax.ShapeDtypeStruct((combine.shape[0], features), bf16),
        in_specs=[in_vmem] * 4 + [anywhere] * 3,
        out_specs=in_vmem,
        scratch_shapes=[
            pltpu.VMEM((units, features), bf16),
            pltpu.VMEM((units, features), bf16),
            pltpu.VMEM((units, features), bf16),
            pltpu.VMEM((2 * size, features), bf16),
            pltpu.VMEM((3, 4 * size, features), bf16),
            pltpu.VMEM((2 * size, features), bf16),
            pltpu.VMEM((2 * size, features), bf16),
            pltpu.VMEM((3, 4 * size, features), bf16),
            pltpu.VMEM((2 * size, features), bf16),
            pltpu.VMEM((size, features), bf16),
            pltpu.VMEM((3, 2 * size, features), bf16),
            pltpu.VMEM((size, features), bf16),
            pltpu.VMEM((4, 2, 3 * chunk, features), bf16),
            pltpu.VMEM((5, 2, chunk, features), bf16),
            pltpu.VMEM((4 * size, units), bf16),
            pltpu.VMEM((STEPS, columns, CAP, features), bf16),
            pltpu.VMEM((3, columns, CAP, features), bf16),
            pltpu.VMEM((3, columns, CAP, features), bf16),
            pltpu.VMEM((3, columns, CAP, features), bf16),
            dma((9,)),
            dma((3, columns)),
            dma((3, columns)),
            dma((3, columns)),
            dma((3, columns)),
            dma((4, 2, 3)),
            dma((4, 2, 3)),
            dma((5, 2, 4)),
            dma((5, 2, 4)),
            dma((5, 2)),
            dma((5, 2)),
            dma((5, 2)),
            dma((5, 2)),
            dma((5, 2)),
            dma((5, 2)),
            dma((4, 2, 3)),
            dma((4, 2, 3)),
        ],
        compiler_params=pltpu.CompilerParams(
            collective_id=0, has_side_effects=True, vmem_limit_bytes=60 * 1024 * 1024
        ),
        name="experts",
    )(attended, hidden_in, selector, combine, gate_weight, up_weight, down_weight)


def body(
    columns,
    hidden_in,
    queries,
    new_entries,
    request_cache_rows,
    lengths,
    expert_ids,
    route_weights,
    gate_weight,
    up_weight,
    down_weight,
):
    attended, selector, combine = attend(
        queries, new_entries, request_cache_rows, lengths, expert_ids, route_weights
    )
    mixture = run_experts(
        columns, attended, hidden_in, selector, combine, gate_weight, up_weight, down_weight
    )
    return attended, mixture.reshape(hidden_in.shape)


def solution(mesh):
    columns = mesh.shape["dev"] // LANE
    placed = (
        P(None, ("sec", "dev"), None),
        P(None, ("sec", "dev"), None),
        P(None, ("sec", "dev"), None),
        P(("sec", "dev"), None, None),
        P(("sec", "dev")),
        P(None, ("sec", "dev"), None),
        P(None, ("sec", "dev"), None),
        P("sec", "dev", None),
        P("sec", "dev", None),
        P("sec", "dev", None),
    )
    return jax.shard_map(
        functools.partial(body, columns),
        mesh=mesh,
        in_specs=placed,
        out_specs=(P(None, ("sec", "dev"), None), P(None, ("sec", "dev"), None)),
        check_vma=False,
    )
```

```python
import functools
import math

import jax
import jax.numpy as jnp
from jax import lax
from jax.experimental import pallas as pl
from jax.experimental.pallas import tpu as pltpu
from jax.sharding import PartitionSpec as P

QUERY_HEADS = 48
KEY_VALUE_HEADS = 8
HEAD_SIZE = 128
E = 8
LONGEST_LENGTH = 192
CAP = 2
STEPS = 2
GROUP = QUERY_HEADS // KEY_VALUE_HEADS
PADDED_GROUP = 8
RING = 8
LANE = 2 * RING
MESH = pl.DeviceIdType.MESH
CONTRACT_LAST = (((1,), (1,)), ((), ()))


def attend_kernel(
    lengths_ref,
    experts_ref,
    weights_ref,
    q_ref,
    fresh_ref,
    cache_ref,
    out_ref,
    selector_ref,
    combine_ref,
    cache,
    q_rows,
    out_rows,
    sem,
):
    requests = cache.shape[0]
    rows = STEPS * PADDED_GROUP
    key_width = KEY_VALUE_HEADS * HEAD_SIZE
    scale = 1.0 / math.sqrt(HEAD_SIZE)
    loads = [
        pltpu.make_async_copy(cache_ref.at[r], cache.at[r], sem.at[r]) for r in range(requests)
    ]
    for load in loads:
        load.start()

    def head_lanes(head, i):
        return pl.ds((head * GROUP + i) * HEAD_SIZE, HEAD_SIZE)

    q_rows[...] = jnp.zeros_like(q_rows)
    for head in range(KEY_VALUE_HEADS):
        for t in range(STEPS):
            for i in range(GROUP):
                at = pl.ds((t * PADDED_GROUP + i) * requests, requests)
                q_rows[head, at] = q_ref[t, :, head_lanes(head, i)].astype(jnp.float32)

    slots, tokens = selector_ref.shape
    slot_at = lax.broadcasted_iota(jnp.int32, (slots, tokens), 0)
    token_at = lax.broadcasted_iota(jnp.int32, (slots, tokens), 1)
    row_at = lax.broadcasted_iota(jnp.int32, combine_ref.shape, 0)
    column_at = lax.broadcasted_iota(jnp.int32, combine_ref.shape, 1)
    selector = jnp.zeros((slots, tokens), jnp.float32)
    combine = jnp.zeros(combine_ref.shape, jnp.float32)
    for t in range(STEPS):
        named = []
        for r in range(requests):
            token = t * requests + r
            for j in range(2):
                expert = experts_ref[t, j, r]
                rank = jnp.int32(0)
                for earlier in named:
                    rank = rank + (earlier == expert).astype(jnp.int32)
                named.append(expert)
                slot = expert * CAP + rank
                selector = jnp.where(
                    (slot_at == slot + t * E * CAP) & (token_at == token), 1.0, selector
                )
                if t == 0:
                    here = (column_at == slot) | (column_at == slot + E * CAP)
                else:
                    here = column_at == slot + 2 * E * CAP
                combine = jnp.where(here & (row_at == token), weights_ref[t, j, r], combine)
    selector_ref[...] = selector.astype(jnp.bfloat16)
    combine_ref[...] = combine

    every = KEY_VALUE_HEADS * rows
    place = lax.broadcasted_iota(jnp.int32, (every, LONGEST_LENGTH), 1)
    second = (lax.broadcasted_iota(jnp.int32, (every, 1), 0) // PADDED_GROUP) % STEPS == 1
    for r in range(requests):
        of_request = pl.ds(r, rows, stride=requests)
        fresh_keys, fresh_values = [], []
        for t in range(STEPS):
            entry = fresh_ref[t, pl.ds(r, 1), :].astype(jnp.float32)
            fresh_keys.append(entry[:, :key_width])
            fresh_values.append(entry[:, key_width:])
        loads[r].wait()
        past, fresh = [], [[] for t in range(STEPS)]
        for head in range(KEY_VALUE_HEADS):
            lanes = slice(head * HEAD_SIZE, (head + 1) * HEAD_SIZE)
            wide = q_rows[head, of_request, :]
            past.append(
                lax.dot_general(
                    wide.astype(jnp.bfloat16),
                    cache[r, :, lanes],
                    CONTRACT_LAST,
                    preferred_element_type=jnp.float32,
                )
            )
            for t in range(STEPS):
                fresh[t].append(jnp.sum(wide * fresh_keys[t][:, lanes], axis=1, keepdims=True))
        past = jnp.concatenate(past, axis=0) * scale
        past = jnp.where(place < lengths_ref[r], past, -jnp.inf)
        fresh = [jnp.concatenate(part, axis=0) * scale for part in fresh]
        fresh[1] = jnp.where(second, fresh[1], -jnp.inf)
        top = jnp.maximum(jnp.max(past, axis=1, keepdims=True), jnp.maximum(fresh[0], fresh[1]))
        past = jnp.exp(past - top)
        fresh = [jnp.exp(part - top) for part in fresh]
        total = jnp.sum(past, axis=1, keepdims=True) + (fresh[0] + fresh[1])
        past = (past / total).astype(jnp.bfloat16)
        fresh = [(part / total).astype(jnp.bfloat16).astype(jnp.float32) for part in fresh]
        for head in range(KEY_VALUE_HEADS):
            lanes = slice(head * HEAD_SIZE, (head + 1) * HEAD_SIZE)
            values = slice(key_width + head * HEAD_SIZE, key_width + (head + 1) * HEAD_SIZE)
            here = slice(head * rows, (head + 1) * rows)
            mixed = jnp.dot(past[here], cache[r, :, values], preferred_element_type=jnp.float32)
            for t in range(STEPS):
                mixed = mixed + fresh[t][here] * fresh_values[t][:, lanes]
            out_rows[head, of_request, :] = mixed
    for head in range(KEY_VALUE_HEADS):
        for t in range(STEPS):
            for i in range(GROUP):
                at = pl.ds((t * PADDED_GROUP + i) * requests, requests)
                out_ref[t, :, head_lanes(head, i)] = out_rows[head, at].astype(jnp.bfloat16)


def attend(queries, new_entries, request_cache_rows, lengths, expert_ids, route_weights):
    steps, requests, features = queries.shape
    rows = STEPS * PADDED_GROUP * requests
    in_vmem = pl.BlockSpec(memory_space=pltpu.VMEM)
    in_smem = pl.BlockSpec(memory_space=pltpu.SMEM)
    return pl.pallas_call(
        attend_kernel,
        out_shape=(
            jax.ShapeDtypeStruct(queries.shape, jnp.bfloat16),
            jax.ShapeDtypeStruct((STEPS * E * CAP, STEPS * requests), jnp.bfloat16),
            jax.ShapeDtypeStruct((STEPS * requests, 3 * E * CAP), jnp.float32),
        ),
        in_specs=[in_smem] * 3 + [in_vmem] * 2 + [pl.BlockSpec(memory_space=pl.ANY)],
        out_specs=(in_vmem,) * 3,
        scratch_shapes=[
            pltpu.VMEM(request_cache_rows.shape, jnp.bfloat16),
            pltpu.VMEM((KEY_VALUE_HEADS, rows, HEAD_SIZE), jnp.float32),
            pltpu.VMEM((KEY_VALUE_HEADS, rows, HEAD_SIZE), jnp.float32),
            pltpu.SemaphoreType.DMA((requests,)),
        ],
        name="attend",
    )(
        lengths,
        expert_ids.transpose(0, 2, 1),
        route_weights.transpose(0, 2, 1),
        queries,
        new_entries,
        request_cache_rows,
    )


FIRST, AGAIN, OWN, CROSSED = 0, 1, 2, 3


def experts_kernel(
    columns,
    attended_ref,
    hidden_ref,
    selector_ref,
    combine_ref,
    gate_ref,
    up_ref,
    down_ref,
    out_ref,
    gate,
    up,
    down,
    rows_0,
    rows_mid,
    rows_4,
    part_0,
    part_mid,
    part_4,
    other_0,
    other_mid,
    other_4,
    ring,
    crossed,
    hidden,
    slot_out,
    slot_in,
    sum_out,
    sum_in,
    load_sem,
    slot_send,
    slot_recv,
    sum_send,
    sum_recv,
    gather_send,
    gather_recv,
    share_send,
    share_recv,
    cross_send,
    cross_recv,
    pair_send,
    pair_recv,
    return_send,
    return_recv,
    reduce_send,
    reduce_recv,
):
    chunk = columns * CAP
    size = 4 * chunk
    features = hidden_ref.shape[-1]
    narrow = min(512, features)
    wide = min(1024, features)
    section = lax.axis_index("sec")
    device = lax.axis_index("dev")
    lane = device % LANE
    column, z, core = device // LANE, lane // 2, device % 2

    def at_z(where):
        return (section, column * LANE + ((where + RING) % RING) * 2 + core)

    sign = 1 - 2 * core
    onward = (at_z(z + sign), at_z(z - sign))
    back = (onward[1], onward[0])
    partner = (section, device + 1 - 2 * core)
    opposite = (1 - section, device)

    def remote(source, target, send_sem, recv_sem, where):
        return pltpu.make_async_remote_copy(
            src_ref=source,
            dst_ref=target,
            send_sem=send_sem,
            recv_sem=recv_sem,
            device_id=where,
            device_id_type=MESH,
        )

    loads = [
        pltpu.make_async_copy(gate_ref.at[0], gate, load_sem.at[0]),
        pltpu.make_async_copy(up_ref.at[0], up, load_sem.at[1]),
        pltpu.make_async_copy(down_ref.at[0], down, load_sem.at[2]),
    ]
    for load in loads:
        load.start()
    in_plane = [
        (where, ((column + offset) % columns) * LANE + lane)
        for where in (section, 1 - section)
        for offset in range(columns)
    ][1:]
    barrier = pltpu.get_barrier_semaphore()
    greeted = onward + (partner,) + tuple(in_plane)
    for where in greeted:
        pl.semaphore_signal(barrier, inc=1, device_id=where, device_id_type=MESH)
    sends = []

    def start(copy):
        copy.start()
        sends.append(copy)

    def exchange(c, source, target, send_sem, recv_sem, local_sem):
        there = 1 - section if c == AGAIN else section
        copies = []
        for offset in range(columns):
            peer = (column + offset) % columns
            if c != AGAIN and offset == 0:
                copy = pltpu.make_async_copy(source.at[peer], target.at[c, column], local_sem)
                copy.start()
                copies.append((copy, copy.wait))
                continue
            copy = remote(
                source.at[peer],
                target.at[c, column],
                send_sem.at[c, offset],
                recv_sem.at[c, offset],
                (there, peer * LANE + lane),
            )
            start(copy)
            copies.append((copy, copy.wait_recv))
        return [wait for copy, wait in copies]

    def block_at(buffers, k, direction, c, of_partner=0):
        at = of_partner * size + c * chunk
        if k == 0:
            return buffers[0].at[pl.ds(at, chunk)]
        if k == 4:
            return buffers[2].at[pl.ds(at, chunk)]
        return buffers[1].at[k - 1, pl.ds(direction * 2 * size + at, chunk)]

    rows_at = functools.partial(block_at, (rows_0, rows_mid, rows_4))
    part_at = functools.partial(block_at, (part_0, part_mid, part_4))

    def gather(k, direction, c):
        return remote(
            rows_at(k - 1, direction, c),
            rows_at(k, direction, c),
            gather_send.at[k - 1, direction, c],
            gather_recv.at[k - 1, direction, c],
            onward[direction],
        )

    def share(k, direction, c):
        return remote(
            rows_at(k, direction, c),
            rows_at(k, direction, c, 1),
            share_send.at[k, direction, c],
            share_recv.at[k, direction, c],
            partner,
        )

    def cross(k, direction):
        return remote(
            rows_at(k, direction, OWN),
            rows_at(k, direction, CROSSED),
            cross_send.at[k, direction],
            cross_recv.at[k, direction],
            opposite,
        )

    def ringed(k):
        if k == 0:
            return []
        if k == 4:
            return [(1, OWN), (0, FIRST), (0, AGAIN)]
        return [(d, c) for c in (OWN, FIRST, AGAIN) for d in (0, 1)]

    def directions(k):
        return (0, 1) if 0 < k < 4 else (0,)

    def home(k, direction):
        return direction if 0 < k < 4 else 0

    def multiply_in(rows):
        count = rows.shape[0]

        x = rows[...]
        value = lax.dot_general(x, gate[...], CONTRACT_LAST, preferred_element_type=jnp.float32)
        value = value / (1.0 + jnp.exp(-value))
        value = value * lax.dot_general(
            x, up[...], CONTRACT_LAST, preferred_element_type=jnp.float32
        )
        hidden[pl.ds(0, count)] = value.astype(jnp.bfloat16)

    def multiply_out(part):
        count = part.shape[0]

        def output_step(i, carry):
            at = pl.ds(pl.multiple_of(i * wide, wide), wide)
            part[:, at] = jnp.dot(
                hidden[pl.ds(0, count)], down[:, at], preferred_element_type=jnp.float32
            ).astype(jnp.bfloat16)
            return carry

        lax.fori_loop(0, features // wide, output_step, 0)

    def pair(k, direction):
        if k == 0:
            source, target = part_0.at[pl.ds(size, size)], other_0
        elif k == 4:
            source, target = part_4.at[pl.ds(size, size)], other_4
        else:
            source = part_mid.at[k - 1, pl.ds(direction * 2 * size + size, size)]
            target = other_mid.at[k - 1, pl.ds(direction * size, size)]
        return remote(
            source, target, pair_send.at[k, direction], pair_recv.at[k, direction], partner
        )

    def other_at(k, direction, c):
        if k == 0:
            return other_0.at[pl.ds(c * chunk, chunk)]
        if k == 4:
            return other_4.at[pl.ds(c * chunk, chunk)]
        return other_mid.at[k - 1, pl.ds(direction * size + c * chunk, chunk)]

    def cross_back(k, direction):
        return remote(
            part_at(k, direction, CROSSED),
            crossed.at[k, direction],
            return_send.at[k, direction],
            return_recv.at[k, direction],
            opposite,
        )

    def ring_at(k, direction, c):
        return ring.at[k, direction, pl.ds(c * chunk, chunk)]

    def reduce(k, direction, c):
        return remote(
            part_at(k, direction, c),
            ring_at(k - 1, direction, c),
            reduce_send.at[k - 1, direction, c],
            reduce_recv.at[k - 1, direction, c],
            back[direction],
        )

    def add(target, sources):
        def step(i, carry):
            at = pl.ds(pl.multiple_of(i * narrow, narrow), narrow)
            total = sources[0][:, at].astype(jnp.float32)
            for source in sources[1:]:
                total = total + source[:, at].astype(jnp.float32)
            target[:, at] = total.astype(jnp.bfloat16)
            return carry

        lax.fori_loop(0, features // narrow, step, 0)

    def send_crossed_sums(k):
        for direction in directions(k):
            pair(k, direction).wait_recv()
            target = part_at(k, direction, CROSSED)
            add(target, [target, other_at(k, direction, CROSSED)])
            start(cross_back(k, direction))

    def send_sums(k, direction, c, from_ring=True):
        sources = [part_at(k, direction, c), other_at(k, direction, c)]
        if c == OWN:
            cross_back(k, home(k, direction)).wait_recv()
            sources.append(crossed.at[k, home(k, direction)])
        if from_ring:
            reduce(k + 1, direction, c).wait_recv()
            sources.append(ring_at(k, direction, c))
        add(sources[0], sources)
        start(reduce(k, direction, c))

    def take_in(k, arrivals):
        for direction, c in arrivals:
            gather(k, direction, c).wait_recv()
            if k < 3 or (k == 3 and (direction, c) in ringed(4)):
                start(gather(k + 1, direction, c))
            if c == OWN:
                start(cross(k, home(k, direction)))
            start(share(k, home(k, direction), c))

    def work_on(k):
        for direction in directions(k):
            cross(k, direction).wait_recv()
            start(share(k, direction, CROSSED))
        for direction in directions(k):
            for c in range(4):
                share(k, direction, c).wait_recv()
        multiply_in(rows_0 if k == 0 else rows_4 if k == 4 else rows_mid.at[k - 1])

    def finish(k):
        multiply_out(part_0 if k == 0 else part_4 if k == 4 else part_mid.at[k - 1])
        for direction in directions(k):
            start(pair(k, direction))

    residual_sum = jnp.concatenate(
        [
            hidden_ref[t].astype(jnp.float32) + attended_ref[t].astype(jnp.float32)
            for t in range(STEPS)
        ],
        axis=0,
    )
    mean_square = jnp.mean(residual_sum * residual_sum, axis=-1, keepdims=True)
    normed = (residual_sum * lax.rsqrt(mean_square + 1e-05)).astype(jnp.bfloat16)
    slots = jnp.dot(selector_ref[...], normed, preferred_element_type=jnp.float32)
    slots = slots.astype(jnp.bfloat16)
    for t in range(STEPS):
        for e in range(columns):
            at = CAP * (t * columns + e)
            slot_out[t, e] = slots[at : at + CAP]
    pl.semaphore_wait(barrier, len(greeted))
    arrivals = {
        c: exchange(
            c, slot_out.at[1 if c == OWN else 0], slot_in, slot_send, slot_recv, load_sem.at[3 + c]
        )
        for c in (OWN, FIRST, AGAIN)
    }

    for c in (OWN, FIRST, AGAIN):
        for wait in arrivals[c]:
            wait()
        for j in range(columns):
            rows_0[pl.ds(c * chunk + CAP * j, CAP)] = slot_in[c, j]
        for direction in range(2):
            start(gather(1, direction, c))
        if c == OWN:
            start(cross(0, 0))
        start(share(0, 0, c))

    take_in(1, ringed(1)[:2])
    for load in loads:
        load.wait()
    for k in range(1, 4):
        if k > 1:
            take_in(k, ringed(k)[:2])
        work_on(k - 1)
        take_in(k, ringed(k)[2:4])
        finish(k - 1)
        take_in(k, ringed(k)[4:])
    take_in(4, ringed(4)[:1])
    work_on(3)
    finish(3)
    send_crossed_sums(3)
    take_in(4, ringed(4)[1:])
    for direction, c in ((1, FIRST), (1, AGAIN), (0, OWN)):
        send_sums(3, direction, c, from_ring=False)
    work_on(4)
    finish(4)

    send_crossed_sums(4)
    send_sums(4, 0, FIRST, from_ring=False)
    send_sums(4, 0, AGAIN, from_ring=False)
    send_sums(4, 1, OWN, from_ring=False)
    send_crossed_sums(2)
    for c, direction in ((FIRST, 0), (AGAIN, 0), (OWN, 1)):
        send_sums(3, direction, c)
    send_crossed_sums(1)
    for k in (2, 1):
        for i in range(3):
            send_sums(k, 0, (OWN, FIRST, AGAIN)[i])
            send_sums(k, 1, (FIRST, AGAIN, OWN)[i])
        if k == 2:
            send_crossed_sums(0)
    arrivals = []
    for c in (FIRST, AGAIN, OWN):
        at = pl.ds(c * chunk, chunk)
        sources = [part_0.at[at], other_0.at[at]]
        if c == OWN:
            cross_back(0, 0).wait_recv()
            sources.append(crossed.at[0, 0])
        for direction in range(2):
            reduce(1, direction, c).wait_recv()
            sources.append(ring_at(0, direction, c))
        add(part_0.at[at], sources)
        for j in range(columns):
            sum_out[c, j] = part_0[pl.ds(c * chunk + CAP * j, CAP)]
        arrivals += exchange(c, sum_out.at[c], sum_in, sum_send, sum_recv, load_sem.at[6 + c])
    for wait in arrivals:
        wait()
    for copy in sends:
        copy.wait_send()
    for c in (FIRST, AGAIN, OWN):
        for j in range(columns):
            part_4[pl.ds(c * chunk + CAP * j, CAP)] = sum_in[c, j]

    weights = combine_ref[...]
    parts = []
    for _ in range(3):
        part = weights.astype(jnp.bfloat16)
        weights = weights - part.astype(jnp.float32)
        parts.append(part)

    def mix_step(i, carry):
        at = pl.ds(pl.multiple_of(i * wide, wide), wide)
        rows = part_4[pl.ds(0, 3 * chunk), at]
        mixture = jnp.dot(parts[2], rows, preferred_element_type=jnp.float32)
        for part in (parts[1], parts[0]):
            mixture = mixture + jnp.dot(part, rows, preferred_element_type=jnp.float32)
        out_ref[:, at] = mixture.astype(jnp.bfloat16)
        return carry

    lax.fori_loop(0, features // wide, mix_step, 0)


def run_experts(
    columns, attended, hidden_in, selector, combine, gate_weight, up_weight, down_weight
):
    features = hidden_in.shape[-1]
    chunk = columns * CAP
    size = 4 * chunk
    units = gate_weight.shape[1]
    bf16 = jnp.bfloat16
    anywhere = pl.BlockSpec(memory_space=pl.ANY)
    in_vmem = pl.BlockSpec(memory_space=pltpu.VMEM)
    dma = pltpu.SemaphoreType.DMA
    return pl.pallas_call(
        functools.partial(experts_kernel, columns),
        out_shape=jax.ShapeDtypeStruct((combine.shape[0], features), bf16),
        in_specs=[in_vmem] * 4 + [anywhere] * 3,
        out_specs=in_vmem,
        scratch_shapes=[
            pltpu.VMEM((units, features), bf16),
            pltpu.VMEM((units, features), bf16),
            pltpu.VMEM((units, features), bf16),
            pltpu.VMEM((2 * size, features), bf16),
            pltpu.VMEM((3, 4 * size, features), bf16),
            pltpu.VMEM((2 * size, features), bf16),
            pltpu.VMEM((2 * size, features), bf16),
            pltpu.VMEM((3, 4 * size, features), bf16),
            pltpu.VMEM((2 * size, features), bf16),
            pltpu.VMEM((size, features), bf16),
            pltpu.VMEM((3, 2 * size, features), bf16),
            pltpu.VMEM((size, features), bf16),
            pltpu.VMEM((4, 2, 3 * chunk, features), bf16),
            pltpu.VMEM((5, 2, chunk, features), bf16),
            pltpu.VMEM((4 * size, units), bf16),
            pltpu.VMEM((STEPS, columns, CAP, features), bf16),
            pltpu.VMEM((3, columns, CAP, features), bf16),
            pltpu.VMEM((3, columns, CAP, features), bf16),
            pltpu.VMEM((3, columns, CAP, features), bf16),
            dma((9,)),
            dma((3, columns)),
            dma((3, columns)),
            dma((3, columns)),
            dma((3, columns)),
            dma((4, 2, 3)),
            dma((4, 2, 3)),
            dma((5, 2, 4)),
            dma((5, 2, 4)),
            dma((5, 2)),
            dma((5, 2)),
            dma((5, 2)),
            dma((5, 2)),
            dma((5, 2)),
            dma((5, 2)),
            dma((4, 2, 3)),
            dma((4, 2, 3)),
        ],
        compiler_params=pltpu.CompilerParams(
            collective_id=0, has_side_effects=True, vmem_limit_bytes=60 * 1024 * 1024
        ),
        name="experts",
    )(attended, hidden_in, selector, combine, gate_weight, up_weight, down_weight)


def body(
    columns,
    hidden_in,
    queries,
    new_entries,
    request_cache_rows,
    lengths,
    expert_ids,
    route_weights,
    gate_weight,
    up_weight,
    down_weight,
):
    attended, selector, combine = attend(
        queries, new_entries, request_cache_rows, lengths, expert_ids, route_weights
    )
    mixture = run_experts(
        columns, attended, hidden_in, selector, combine, gate_weight, up_weight, down_weight
    )
    return attended, mixture.reshape(hidden_in.shape)


def solution(mesh):
    columns = mesh.shape["dev"] // LANE
    placed = (
        P(None, ("sec", "dev"), None),
        P(None, ("sec", "dev"), None),
        P(None, ("sec", "dev"), None),
        P(("sec", "dev"), None, None),
        P(("sec", "dev")),
        P(None, ("sec", "dev"), None),
        P(None, ("sec", "dev"), None),
        P("sec", "dev", None),
        P("sec", "dev", None),
        P("sec", "dev", None),
    )
    return jax.shard_map(
        functools.partial(body, columns),
        mesh=mesh,
        in_specs=placed,
        out_specs=(P(None, ("sec", "dev"), None), P(None, ("sec", "dev"), None)),
        check_vma=False,
    )
```
